512 devices in a mesh: expert: 8 (over y), basis: 64 (over x, z, core).
Axes of the slice: x: 4, y: 8, z: 8, core: 2. Of those that a mesh axis runs over, the one named last changes fastest.
Arguments:
- out_grads: bfloat16 [1024, 8192], P('expert', 'basis'), may hold values from -6 to 6
- in_acts: bfloat16 [1024, 3072], P('expert', 'basis'), may hold values from -6 to 6
- routes: int32 [1024, 2], P('expert'), may hold values from 0 to 7, all different within a row; in each aligned block of 128 rows (0 to 127, 128 to 255, ...) at most 40 rows name the same one
- seq_ids: int32 [1024], P('expert'), may hold values from 0 to 127, never falling along the last dimension, each value on 1 to 16 neighbouring positions
- query_out: bfloat16 [8, 128, 8192], P('expert', None, 'basis'), may hold values from -6 to 6
- query_in: bfloat16 [8, 128, 3072], P('expert', None, 'basis'), may hold values from -6 to 6
- out_basis: bfloat16 [8, 8192, 8192], P('expert', 'basis'), may hold values from -0.0625 to 0.0625
- in_basis: bfloat16 [8, 3072, 3072], P('expert', 'basis'), may hold values from -0.109375 to 0.109375
- eigvals: float32 [8, 8192, 3072], P('expert', 'basis'), may hold values from 0.05 to 5
Outputs:
- influence: float32 [8, 128], P(None, 'basis')
The draws below stay inside these ranges and needn't reach their ends.
Inputs may be any that keep to these rules, and one draw needn't show every extreme that they name: Each token names 2 different experts. Among the routes of the 128 tokens of one group, no expert is named more than 40 times, a bound that some group reaches. `seq_ids`: never falling along the tokens; every sequence has 1 to 16 tokens and one has exactly 16.
All inputs are finite; a program needn't handle non-finite values.
Results may differ from the reference program's by a relative error of at most 0.0045.
Values may be sent and summed in bfloat16 or wider, within the bound.
A program may use at most 128 MiB of HBM per device.

```python
import math
import jax
import jax.numpy as jnp
import numpy as np
from jax import lax

D = 3072
FF = 8192
E = 8
TOP = 2
TOK_GROUP = 128
CAP = 40
QUERIES = 8
QRANK = 16
TOKENS = 1024
SEQS = 128
SEG_MOST = 16
N_EXPERT = 8


def steps_of(stream_key, shape, pieces, smallest, largest):
    gain = 1.0
    for axis_at, shards_of in pieces:
        draws = jax.random.uniform(jax.random.fold_in(jax.random.fold_in(stream_key, 6), axis_at), (shards_of,), jnp.float32, smallest / len(pieces), largest / len(pieces))
        gain = gain * jnp.repeat(jnp.exp(draws), shape[axis_at] // shards_of).reshape((-1,) + (1,) * (len(shape) - 1 - axis_at))
    return gain


def split_up(number_of, total, bound, lean):
    weights = [(1 << 20) // math.isqrt(standing ** lean) + 1 for standing in range(2, number_of + 1)]
    rest, given = total - bound - (number_of - 1), [1] * (number_of - 1)
    while rest > 0:
        candidates = [i for i in range(number_of - 1) if given[i] < bound]
        pool, left = sum([weights[i] for i in candidates]), rest
        for i in candidates:
            addition = min(bound - given[i], max(1, left * weights[i] // pool), rest)
            given[i] = given[i] + addition
            rest = rest - addition
    return np.array([bound] + given)


def uneven(own_key, number_of, total, limit, skew):
    if number_of == 2:
        one = jax.random.randint(own_key, (), max(1, total - limit), min(limit, total - 1) + 1)
        return jnp.stack([one, total - one])
    tallies = jnp.asarray(split_up(number_of, total, limit, skew), jnp.int32)
    twos = (number_of - 1) // 2
    giver, sink = tallies[1:1 + 2 * twos:2], tallies[2:2 + 2 * twos:2]
    slack = jnp.minimum(giver - 1, limit - sink)
    moved = jax.random.randint(jax.random.fold_in(own_key, 1), (twos,), 0, 1 << 20) % (slack + 1)
    tallies = tallies.at[1:1 + 2 * twos:2].set(giver - moved).at[2:2 + 2 * twos:2].set(sink + moved)
    return tallies[jax.random.permutation(jax.random.fold_in(own_key, 2), number_of)]


def assign_block(key, own, number, rows, amount, top, bound, lean):
    order = jax.random.permutation(key, amount)
    crowded, ordinary = shares(amount, rows * top, bound, lean, True), shares(amount, rows * top, bound, lean, False)
    places = jnp.arange(amount)

    def named(tallies, rotation):
        used = int((tallies > 0).sum())
        fixed = max(1, used // 4)
        passed = fixed + (places - fixed + rotation * (used - fixed)) % max(1, amount - fixed)
        return jnp.zeros((amount,), jnp.int32).at[order[jnp.where(places < fixed, places, passed)]].set(jnp.asarray(tallies, jnp.int32))

    tallies = jnp.where(number % 4 == 0, named(crowded, number // 4), named(ordinary, number - number // 4 - 1))
    mixed = jax.random.permutation(jax.random.fold_in(own, 3), amount)
    source_of, sink = mixed[0:amount // 2 * 2:2], mixed[1:amount // 2 * 2:2]
    slack = jnp.minimum(tallies[source_of] - 1, bound - tallies[sink]) // 2
    slack = jnp.where((source_of == order[0]) | (sink == order[0]) | (tallies[sink] == 0), 0, jnp.maximum(slack, 0))
    passed = jax.random.randint(jax.random.fold_in(own, 4), (amount // 2,), 0, 1 << 20) % (slack + 1)
    tallies = tallies.at[source_of].add(-passed).at[sink].add(passed)
    items = jnp.searchsorted(jnp.cumsum(tallies), jnp.arange(rows * top), side="right").astype(jnp.int32)
    table = items.reshape(top, rows).T
    table = table[jax.random.permutation(jax.random.fold_in(own, 1), rows)]
    rotation = jax.random.randint(jax.random.fold_in(own, 2), (rows, 1), 0, top)
    return jnp.take_along_axis(table, (jnp.arange(top)[None, :] + rotation) % top, axis=1)


def shares(number_of, total, limit, slope, full):
    portions = [(1 << 20) // math.isqrt(standing ** slope) + 1 for standing in range(1, number_of + 1)]
    largest = limit if full else min(limit, max(-(-total // number_of), total * portions[0] // sum(portions)))
    least = 1 if total - largest >= number_of - 1 else 0
    holding, rest = [largest] + [least] * (number_of - 1), total - largest - least * (number_of - 1)
    while rest > 0:
        movable = [i for i in range(1, number_of) if holding[i] < largest] or [i for i in range(1, number_of) if holding[i] < limit]
        whole, budget = sum([portions[i] for i in movable]), rest
        for i in movable:
            addition = min(limit - holding[i], max(1, budget * portions[i] // whole), rest)
            holding[i] = holding[i] + addition
            rest = rest - addition
    return np.array(holding)


def centred(own_key, dims, deviation, bound, cuts=(), held_as=jnp.bfloat16):
    values = jax.random.normal(own_key, dims, jnp.float32) * deviation
    if len(cuts) > 0:
        values = steps_of(own_key, dims, cuts, -0.22, 0.18) * values
    return jnp.clip(values, min=-bound, max=bound).astype(held_as)


def setup_inputs(seed: int = 0) -> dict:
    seeds = jax.random.split(jax.random.key(seed), 10)
    out_grads = centred(seeds[0], (TOKENS, FF), 1.0, 6.0, ((0, 8), (1, 64)))
    in_acts = centred(seeds[1], (TOKENS, D), 1.0, 6.0, ((0, 8), (1, 64)))
    routes_keys = jax.random.split(jax.random.fold_in(seeds[2], 1), TOKENS // TOK_GROUP)
    routes_turns = jax.random.permutation(jax.random.fold_in(seeds[2], 3), TOKENS // TOK_GROUP)
    routes = jax.vmap(lambda own, number: assign_block(jax.random.fold_in(seeds[2], 2), own, number, TOK_GROUP, E, TOP, CAP, 2))(routes_keys, routes_turns).reshape((TOKENS, TOP))
    seq_ids = jnp.searchsorted(jnp.cumsum(uneven(seeds[3], SEQS, TOKENS, SEG_MOST, 1)), jnp.arange(TOKENS), side="right").astype(jnp.int32)
    query_out = centred(seeds[4], (E, QUERIES * QRANK, FF), 1.0, 6.0, ((0, 8), (2, 64)))
    query_in = centred(seeds[5], (E, QUERIES * QRANK, D), 1.0, 6.0, ((0, 8), (2, 64)))
    out_basis = centred(seeds[6], (E, FF, FF), FF ** -0.5, 0.0625, ((0, 8), (1, 64)))
    in_basis = centred(seeds[7], (E, D, D), D ** -0.5, 0.109375, ((0, 8), (1, 64)))
    eigvals = jnp.clip(jnp.exp(math.log(5.0) - 4.6051702 * jax.random.uniform(seeds[8], (E, FF, D), jnp.float32) ** steps_of(seeds[8], (E, FF, D), ((0, 8), (1, 64)), -0.2, 0.2)), 0.05, 5.0)
    return {"out_grads": out_grads, "in_acts": in_acts, "routes": routes, "seq_ids": seq_ids, "query_out": query_out, "query_in": query_in, "out_basis": out_basis, "in_basis": in_basis, "eigvals": eigvals}


damping_shift = 0.1

def route_slots(route_rows, experts, capacity):
    flat_routes = route_rows.reshape(-1).astype(jnp.int32)
    onehot_routes = (flat_routes[:, None] == jnp.arange(experts, dtype=jnp.int32)[None, :]).astype(jnp.int32)
    earlier = jnp.cumsum(onehot_routes, axis=0) - onehot_routes
    position = lax.optimization_barrier(jnp.sum(earlier * onehot_routes, axis=1)).astype(jnp.int32)
    destination = (flat_routes * capacity + position).astype(jnp.int32)
    token_of_route = (jnp.arange(flat_routes.shape[0], dtype=jnp.int32) // route_rows.shape[1]).astype(jnp.int32)
    slot_token = jnp.zeros((experts * capacity,), jnp.int32).at[destination].set(token_of_route)
    return (slot_token, destination)

def reference(out_grads, in_acts, routes, seq_ids, query_out, query_in, out_basis, in_basis, eigvals):
    groups = N_EXPERT
    group_routes = routes.reshape(groups, TOK_GROUP, TOP)
    slot_token, destination = jax.vmap(lambda rows_here: route_slots(rows_here, E, CAP))(group_routes)
    global_token = (slot_token + (jnp.arange(groups, dtype=jnp.int32) * TOK_GROUP)[:, None]).astype(jnp.int32)
    global_token = global_token.reshape(groups, E, CAP)
    score_scale = 1.0 / (8.0 * math.sqrt(FF * D * QRANK))
    contract = (((1,), (1,)), ((), ()))

    def per_expert(packed):
        expert_id, qout_here, qin_here, basis_out, basis_in, eig_here = packed
        rows_here = lax.dynamic_index_in_dim(global_token, expert_id, axis=1, keepdims=False).reshape(-1)
        slot_out = jnp.take(out_grads, rows_here, axis=0)
        slot_in = jnp.take(in_acts, rows_here, axis=0)
        tok_out = lax.dot_general(basis_out, slot_out, contract, preferred_element_type=jnp.float32).astype(jnp.bfloat16)
        tok_in = lax.dot_general(basis_in, slot_in, contract, preferred_element_type=jnp.float32).astype(jnp.bfloat16)
        qry_out = lax.dot_general(basis_out, qout_here, contract, preferred_element_type=jnp.float32).astype(jnp.bfloat16)
        qry_in = lax.dot_general(basis_in, qin_here, contract, preferred_element_type=jnp.float32).astype(jnp.bfloat16)
        stack_out = qry_out.reshape(FF, QUERIES, QRANK).transpose(1, 0, 2)
        stack_in = qry_in.reshape(D, QUERIES, QRANK).transpose(1, 0, 2)
        denominator = eig_here + damping_shift
        tok_out_wide = tok_out.astype(jnp.float32)

        def one_query(pair):
            factor_out, factor_in = pair
            gradient = lax.dot_general(factor_out, factor_in, contract, preferred_element_type=jnp.float32)
            conditioned = (gradient / denominator).astype(jnp.bfloat16)
            projected = jnp.dot(conditioned, tok_in, preferred_element_type=jnp.float32)
            return lax.optimization_barrier(jnp.sum(tok_out_wide * projected, axis=0)) * score_scale
        return lax.map(one_query, (stack_out, stack_in))
    slot_scores = lax.map(per_expert, (jnp.arange(E, dtype=jnp.int32), query_out, query_in, out_basis, in_basis, eigvals))
    by_group = slot_scores.reshape(E, QUERIES, groups, CAP).transpose(2, 1, 0, 3).reshape(groups, QUERIES, E * CAP)
    route_scores = jnp.take_along_axis(by_group, destination[:, None, :], axis=2)
    route_scores = route_scores.transpose(1, 0, 2).reshape(QUERIES, groups * TOK_GROUP * TOP)
    route_seq = jnp.repeat(seq_ids, TOP)
    onehot_seq = (jnp.arange(SEQS, dtype=jnp.int32)[:, None] == route_seq[None, :]).astype(jnp.float32)
    return jnp.dot(route_scores, onehot_seq.T, precision=lax.Precision.HIGHEST)
```

```python
import functools
import math

import jax
import jax.numpy as jnp
from jax import lax
from jax.experimental import pallas as pl
from jax.experimental.pallas import tpu as pltpu
from jax.sharding import PartitionSpec as P

D = 3072
FF = 8192
QUERIES = 8
QRANK = 16
NX, NZ, NC = 4, 8, 2
CAP = 40
CAPP = 48
damping_shift = 0.1
F32 = jnp.float32
BF16 = jnp.bfloat16
MESH = pl.DeviceIdType.MESH
NN = (((1,), (0,)), ((), ()))
NT = (((1,), (1,)), ((), ()))


def mm(a, b, dims=NN):
    return lax.dot_general(a, b, dims, preferred_element_type=F32)


def iota(shape, dim):
    return lax.broadcasted_iota(jnp.int32, shape, dim)


def split3(v):
    hi = v.astype(BF16)
    rest = v - hi.astype(F32)
    mid = rest.astype(BF16)
    low = (rest - mid.astype(F32)).astype(BF16)
    return hi, mid, low


class Gather:
    def __init__(self, buf, send, recv, slot, pos, nbr, z_rows, halves, x_rows, flip):
        self.buf, self.send, self.recv, self.slot = buf, send, recv, slot
        self.x, self.z = pos
        self.nbr = nbr
        self.zr, self.halves, self.xr, self.flip = z_rows, halves, x_rows, flip
        self.made = []
        self.live = {}

    def go(self, name, view, to):
        i = len(self.made)
        copy = pltpu.make_async_remote_copy(
            src_ref=view,
            dst_ref=view,
            send_sem=self.send.at[self.slot, i],
            recv_sem=self.recv.at[self.slot, i],
            device_id={"basis": self.nbr[to]},
            device_id_type=MESH,
        )
        copy.start()
        self.made.append(copy)
        self.live[name] = copy

    def got(self, *names):
        for name in names:
            self.live[name].wait_recv()

    def zat(self, d):
        return lax.rem(self.z + d + NZ, NZ)

    def xat(self, d):
        return lax.rem(self.x + d + NX, NX)

    def zblock(self, d, rows):
        return self.buf.at[self.x, self.zat(d), rows]

    def xblock(self, d, rows):
        return self.buf.at[:, self.zat(d), rows]

    def step(self, level):
        zr, xr = self.zr, self.xr
        if level == 0:
            self.go("zr1", self.zblock(0, zr), "z+")
            self.go("zl1", self.zblock(0, zr), "z-")
            self.go("axr", self.zblock(0, xr), "x+")
            self.go("axl", self.zblock(0, xr), "x-")
        elif level == 1:
            self.got("zr1", "zl1")
            self.go("zr2", self.zblock(-1, zr), "z+")
            self.go("zl2", self.zblock(1, zr), "z-")
            self.got("axr", "axl")
            d, to = (1, "x-") if self.flip else (-1, "x+")
            self.go("ax2", self.buf.at[self.xat(d), self.z, xr], to)
        elif level == 2:
            self.got("zr2", "zl2")
            self.go("zr3", self.zblock(-2, zr), "z+")
            self.go("zl3", self.zblock(2, zr), "z-")
            self.got("ax2")
            self.go("bzr1", self.xblock(0, xr), "z+")
            self.go("bzl1", self.xblock(0, xr), "z-")
        elif level == 3:
            self.got("zr3", "zl3")
            self.go("zr4", self.zblock(-3, self.halves[0]), "z+")
            self.go("zl4", self.zblock(3, self.halves[1]), "z-")
            self.got("bzr1", "bzl1")
            self.go("bzr2", self.xblock(-1, xr), "z+")
            self.go("bzl2", self.xblock(1, xr), "z-")
        elif level == 4:
            self.got("zr4", "zl4")
            self.go("xr1", self.buf.at[self.x, :, zr], "x+")
            self.go("xl1", self.buf.at[self.x, :, zr], "x-")
            self.got("bzr2", "bzl2")
            self.go("bzr3", self.xblock(-2, xr), "z+")
            self.go("bzl3", self.xblock(2, xr), "z-")
        elif level == 5:
            self.got("bzr3", "bzl3")
            self.go("bzr4", self.buf.at[pl.ds(0, 2), self.zat(-3), xr], "z+")
            self.go("bzl4", self.buf.at[pl.ds(2, 2), self.zat(3), xr], "z-")
            self.got("xr1", "xl1")
            self.go("xr2", self.buf.at[self.xat(-1), pl.ds(0, 4), zr], "x+")
            self.go("xl2", self.buf.at[self.xat(1), pl.ds(4, 4), zr], "x-")
        elif level == 6:
            self.got("bzr4", "bzl4", "xr2", "xl2")

    def close(self):
        for copy in self.made:
            copy.wait_send()


def kernel(
    og_h, ia_h, rt_h, sq_h, qo_h, qi_h, bo_h, bi_h, eg_h,
    out_ref,
    og, ia, rt, sq, bo, bi, eg,
    qb, ib, tb, rb,
    a2s, a2r,
    sel, bisel, inv, hot,
    pin, pinr, pq, pqr, acc, accr,
    qrot, qit, cond, proj, score,
    reds, redr,
    lsem, gsend, grecv, asend, arecv, dsend, drecv, rsend, rrecv,
):
    e = lax.axis_index("expert")
    b = lax.axis_index("basis")
    c = lax.rem(b, NC)
    z = lax.rem(lax.div(b, NC), NZ)
    x = lax.div(b, NC * NZ)
    n_e = 8

    def at(xx, zz, cc):
        return (lax.rem(xx + NX, NX) * NZ + lax.rem(zz + NZ, NZ)) * NC + cc

    sib = at(x, z, 1 - c)
    nbr = {"x+": at(x + 1, z, c), "x-": at(x - 1, z, c), "z+": at(x, z + 1, c), "z-": at(x, z - 1, c)}
    xc = x * NC + c

    def ypeer(d):
        return {"expert": lax.rem(e + d, n_e)}

    def zpeer(d):
        return {"basis": at(x, z + d, c)}

    def xpeer(d):
        m = lax.rem(xc + d, NX * NC)
        return {"basis": at(lax.div(m, NC), z, lax.rem(m, NC))}

    locals_ = [
        (qo_h, qb.at[x, z]),
        (qi_h, ib.at[x, z, :, pl.ds(0, 128)]),
        (rt_h, rt),
        (og_h, og),
        (ia_h, ia),
        (sq_h, sq),
        (bi_h, bi.at[c]),
        (bo_h, bo.at[c]),
        (eg_h, eg.at[c]),
    ]
    local = [pltpu.make_async_copy(s, d, lsem.at[i]) for i, (s, d) in enumerate(locals_)]
    for copy in local:
        copy.start()

    barrier = pltpu.get_barrier_semaphore()
    for group in (ypeer, zpeer, xpeer):
        for d in range(1, 8):
            pl.semaphore_signal(barrier, inc=1, device_id=group(d), device_id_type=MESH)
    local[0].wait()
    local[1].wait()
    pl.semaphore_wait(barrier, 21)

    def remote(src, dst, ss, rs, to):
        copy = pltpu.make_async_remote_copy(
            src_ref=src, dst_ref=dst, send_sem=ss, recv_sem=rs, device_id=to, device_id_type=MESH
        )
        copy.start()
        return copy

    def to_sibling(i, src, dst):
        return remote(src, dst, dsend.at[i], drecv.at[i], {"basis": sib})

    pos = (x, z)
    ds = pl.ds
    g1 = Gather(qb, gsend, grecv, 0, pos, nbr, ds(0, 80), (ds(0, 48), ds(48, 32)), ds(80, 48), False)
    g2 = Gather(ib, gsend, grecv, 1, pos, nbr, ds(0, 32), (ds(0, 16), ds(16, 16)), ds(32, 16), True)
    g3 = Gather(tb, gsend, grecv, 2, pos, nbr, ds(0, 192), (ds(0, 96), ds(96, 96)), ds(192, 128), False)
    g4 = Gather(rb, gsend, grecv, 3, pos, nbr, ds(0, 32), (ds(0, 16), ds(16, 16)), ds(32, 16), True)

    g1.step(0)
    d_bi = to_sibling(0, bi_h, bi.at[c])
    d_bo = to_sibling(1, bo_h, bo.at[c])
    d_eg = to_sibling(2, eg_h, eg.at[c])

    for i in range(2, 6):
        local[i].wait()
    r = rt[...]
    who = iota((8, 128), 0)
    hit = jnp.logical_or(r[0:1, :] == who, r[1:2, :] == who)
    upper = jnp.where(iota((128, 128), 0) < iota((128, 128), 1), 1.0, 0.0).astype(BF16)
    place = mm(jnp.where(hit, 1.0, 0.0).astype(BF16), upper)
    place = jnp.where(hit, place, -1.0).astype(jnp.int32)
    pick = jnp.where(place[:, None, :] == iota((8, CAPP, 128), 1), 1.0, 0.0)
    pick = pick.reshape(8 * CAPP, 128).astype(BF16)
    rows_out = mm(pick, og[...])
    seq_row = jnp.broadcast_to(sq[...], (16, 128)).astype(F32).astype(BF16)
    in_ext = jnp.concatenate([ia[...], seq_row, jnp.zeros((64, 128), BF16)], axis=0)
    rows_in = mm(pick, in_ext, NT)
    a2s[:, :, 0:128] = rows_out.astype(BF16).reshape(8, CAPP, 128)
    a2s[:, :, 128:256] = rows_in.astype(BF16).reshape(8, CAPP, 128)
    a2a = []
    for d in range(1, 8):
        a2a.append(
            remote(a2s.at[lax.rem(e + d, n_e)], a2r.at[e], asend.at[d - 1], arecv.at[d - 1], ypeer(d))
        )
    a2r[e] = a2s[e]
    g1.step(1)

    w = iota((8, 96, 384), 1) - 48 * c
    want = jnp.logical_and(jnp.logical_and(w >= 0, w < 48), iota((8, 96, 384), 2) == 48 * iota((8, 96, 384), 0) + w)
    sel[...] = jnp.where(want, 1.0, 0.0).reshape(768, 384).astype(BF16)
    g1.step(2)

    dense = jnp.where(
        iota((8, CAP, 8 * CAPP), 2) == CAPP * iota((8, CAP, 8 * CAPP), 0) + iota((8, CAP, 8 * CAPP), 1), 1.0, 0.0
    ).reshape(8 * CAP, 8 * CAPP)
    dense = jnp.concatenate([dense, jnp.zeros((64, 8 * CAPP), F32)], axis=0).astype(BF16)
    for copy in a2a:
        copy.wait_recv()
    rows = mm(dense, a2r[...].reshape(8 * CAPP, 256))
    tb[x, z] = rows[0:320, 0:128].astype(BF16)
    ib[x, z, :, 128:448] = rows[:, 128:256].T[0:48, 0:320].astype(BF16)
    seq_of = rows[0:320, 128 + 48 : 128 + 49]
    hot[...] = jnp.where(seq_of == iota((320, 128), 1).astype(F32), 1.0, 0.0).astype(BF16)
    g2.step(0)
    g1.step(3)
    g2.step(1)
    g1.step(4)
    g2.step(2)
    g3.step(0)

    local[6].wait()
    d_bi.wait_recv()
    for cc in range(2):
        for m in range(4):
            part = mm(bi[cc, :, 768 * m : 768 * (m + 1)], sel[...])
            bisel[48 * cc : 48 * (cc + 1), 384 * m : 384 * (m + 1)] = part.astype(BF16)
    g1.step(5)
    g2.step(3)
    g2.step(4)
    g3.step(1)
    g1.step(6)

    local[7].wait()
    d_bo.wait_recv()

    def basis_cols(p):
        cols = pl.ds(pl.multiple_of(256 * p + 128 * c, 128), 128)
        return jnp.concatenate([bo[0, :, cols], bo[1, :, cols]], axis=0)

    def contract_pair(src, p):
        lhs = jnp.concatenate([basis_cols(2 * p), basis_cols(2 * p + 1)], axis=1)
        xx, zz = lax.div(2 * p, NZ), lax.rem(2 * p, NZ)
        rhs = jnp.concatenate([src[xx, zz], src[xx, zz + 1]], axis=1)
        return mm(lhs, rhs, NT)

    pq[...] = jnp.zeros_like(pq)

    @pl.loop(0, 16)
    def _(p):
        pq[...] += contract_pair(qb, p)

    d_pq = to_sibling(3, pq, pqr)
    g3.step(2)
    g2.step(5)
    g3.step(3)

    local[8].wait()
    d_eg.wait_recv()
    for cc in range(2):
        for m in range(4):
            parts = split3(eg[cc, :, 768 * m : 768 * (m + 1)])
            chosen = mm(parts[0], sel[...]) + mm(parts[1], sel[...]) + mm(parts[2], sel[...])
            inv[128 * cc : 128 * (cc + 1), 384 * m : 384 * (m + 1)] = 1.0 / (chosen + damping_shift)

    g2.step(6)
    part = mm(bisel[...], ib[...].reshape(NX * NZ * 48, 448))
    pin[0] = part[0:48]
    pin[1] = part[48:96]
    d_pin = to_sibling(4, pin.at[1 - c], pinr)
    d_pq.wait_recv()
    qrot[...] = (pq[...] + pqr[...]).astype(BF16)
    d_pin.wait_recv()
    rb[x, z] = (pin[c] + pinr[...]).astype(BF16)
    g4.step(0)
    g3.step(4)
    g4.step(1)
    g4.step(2)
    g4.step(3)
    g4.step(4)
    g3.step(5)
    g4.step(5)
    g4.step(6)

    qit[...] = rb[:, :, :, 0:128].reshape(NX * NZ * 48, 128).astype(F32).T.astype(BF16)

    def one_query(q):
        lane = iota((256, 128), 1)
        mine = jnp.logical_and(lane >= q * QRANK, lane < (q + 1) * QRANK)
        lhs = jnp.where(mine, qrot[...].astype(F32), 0.0).astype(BF16)
        for m in range(4):
            cols = slice(384 * m, 384 * (m + 1))
            cond[:, cols] = (mm(lhs, qit[:, cols]) * inv[:, cols]).astype(BF16)
        proj[q] = mm(cond[...], rb[:, :, :, 128:448].reshape(NX * NZ * 48, 320))

    pl.loop(0, QUERIES)(one_query)

    g3.step(6)
    acc[...] = jnp.zeros_like(acc)

    @pl.loop(0, 16)
    def _(p):
        acc[...] += contract_pair(tb, p)

    d_acc = to_sibling(5, acc, accr)
    d_acc.wait_recv()
    tok = (acc[...] + accr[...]).astype(BF16).astype(F32)
    for q in range(QUERIES):
        score[q : q + 1, :] = jnp.sum(tok * proj[q], axis=0, keepdims=True)
    scale = 1.0 / (8.0 * math.sqrt(FF * D * QRANK))
    parts = split3(score[...] * scale)
    total = mm(parts[0], hot[...]) + mm(parts[1], hot[...]) + mm(parts[2], hot[...])

    sums = []
    for s, group in enumerate((xpeer, zpeer, ypeer)):
        reds[s] = total
        copies = [
            remote(reds.at[s], redr.at[s, d - 1], rsend.at[s, d - 1], rrecv.at[s, d - 1], group(d))
            for d in range(1, 8)
        ]
        sums += copies
        for copy in copies:
            copy.wait_recv()
        for d in range(7):
            total = total + redr[s, d]
    lane = iota((8, 128), 1)
    col0 = jnp.sum(jnp.where(lane == 2 * b, total, 0.0), axis=1, keepdims=True)
    col1 = jnp.sum(jnp.where(lane == 2 * b + 1, total, 0.0), axis=1, keepdims=True)
    out_ref[...] = jnp.concatenate([col0, col1], axis=1)

    for g in (g1, g2, g3, g4):
        g.close()
    for copy in a2a + sums + [d_bi, d_bo, d_eg, d_pq, d_pin, d_acc]:
        copy.wait_send()


def on_device(out_grads, in_acts, routes, seq_ids, query_out, query_in, out_basis, in_basis, eigvals):
    dma = pltpu.SemaphoreType.DMA
    v = pltpu.VMEM
    return pl.pallas_call(
        kernel,
        out_shape=jax.ShapeDtypeStruct((QUERIES, 2), F32),
        in_specs=[pl.BlockSpec(memory_space=pl.ANY)] * 9,
        out_specs=pl.BlockSpec(memory_space=pltpu.VMEM),
        scratch_shapes=[
            v((128, 128), BF16), v((48, 128), BF16), v((2, 128), jnp.int32), v((1, 128), jnp.int32),
            v((2, 128, FF), BF16), v((2, 48, D), BF16), v((2, 128, D), F32),
            v((NX, NZ, 128, 128), BF16), v((NX, NZ, 48, 448), BF16), v((NX, NZ, 320, 128), BF16), v((NX, NZ, 48, 448), BF16),
            v((8, CAPP, 256), BF16), v((8, CAPP, 256), BF16),
            v((768, 384), BF16), v((96, 1536), BF16), v((256, 1536), F32), v((320, 128), BF16),
            v((2, 48, 448), F32), v((48, 448), F32), v((256, 128), F32), v((256, 128), F32), v((256, 320), F32), v((256, 320), F32),
            v((256, 128), BF16), v((128, 1536), BF16), v((256, 1536), BF16), v((QUERIES, 256, 320), F32), v((QUERIES, 320), F32),
            v((3, 8, 128), F32), v((3, 7, 8, 128), F32),
            dma((9,)), dma((4, 23)), dma((4, 23)), dma((7,)), dma((7,)), dma((6,)), dma((6,)), dma((3, 7)), dma((3, 7)),
        ],
        compiler_params=pltpu.CompilerParams(
            collective_id=0, has_side_effects=True, vmem_limit_bytes=52 * 1024 * 1024
        ),
    )(
        out_grads, in_acts.T, routes.T, seq_ids.reshape(1, -1), query_out[0], query_in[0].T,
        out_basis[0], in_basis[0], eigvals[0],
    )


def solution(mesh):
    return jax.shard_map(
        on_device,
        mesh=mesh,
        in_specs=(
            P("expert", "basis"),
            P("expert", "basis"),
            P("expert", None),
            P("expert"),
            P("expert", None, "basis"),
            P("expert", None, "basis"),
            P("expert", "basis", None),
            P("expert", "basis", None),
            P("expert", "basis", None),
        ),
        out_specs=P(None, "basis"),
        check_vma=False,
    )
```

```python
import math

import jax
import jax.numpy as jnp
from jax import lax
from jax.experimental import pallas as pl
from jax.experimental.pallas import tpu as pltpu
from jax.sharding import PartitionSpec as P

D = 3072
FF = 8192
QUERIES = 8
QRANK = 16
NX, NZ, NC, NE = 4, 8, 2, 8
CAP = 40
CAPP = 48
damping_shift = 0.1
F32 = jnp.float32
BF16 = jnp.bfloat16
MESH = pl.DeviceIdType.MESH
NN = (((1,), (0,)), ((), ()))
NT = (((1,), (1,)), ((), ()))

WAYS = {
    1: (True, False, False),
    2: (True, False, False),
    3: (False, False, False),
    4: (True, True, False),
    5: (True, True, True),
}

ORDER = [
    "a2a", "1zr2", "1zl1", "1axl", "1ax2", "1zl2", "deg", "1axr", "1bl1", "1zr1", "dbi", "1br1", "inv1", "1zr3",
    "1zl4", "1zl3", "1zr4", "own2", "2zr2", "2zl2", "2axr", "2axl", "3axl", "3zl1", "3zr1", "2ax2", "3ax2", "2zl1",
    "bis0", "1bl2", "2zr1", "inv5", "1br2", "1xl1", "3axr", "1xr1", "bis1", "2zl3", "2zr3", "2br1", "inv3", "2bl1",
    "2zr4", "3zr2", "2zl4", "3bl1", "1bl3", "3zl2", "1br3", "inv2", "2xr1", "3br1", "2xl1", "2bl2", "inv7", "2br2",
    "dbo", "3zl3", "3zr3", "1xl2", "1xr2", "2br3", "1bl4", "inv0", "1br4", "2bl3", "2xr2", "3bl2", "2xl2", "3br2",
    "3zr4", "3zl4", "qi", "dpqi", "2br4", "2bl4", "3xr1", "3xl1", "own4", "4zr2", "4axl", "4zr1", "4zl2", "4zl1",
    "3bl3", "3br3", "4ax2", "4axr", "rin", "drt", "4zr3", "inv4", "own5", "5axr", "5zr2", "5zl1", "5axl", "4zl3",
    "5zr1", "4zl4", "5zl2", "4zr4", "qo0", "4br2", "5ax2", "3bl4", "3br4", "qo1", "5zr4", "4bl2", "4br1", "5zr3",
    "4xr1", "4xl1", "5zl4", "5bl1", "inv6", "5zl3", "5br2", "5xr1_2", "5xl1_1", "4br4", "5bl2", "5xl1_-1", "5xr1_0",
    "5xr1_-2", "5xl1_-2", "5xl1_2", "4br3", "acc0", "5xl1_-3", "5xr1_4", "5xr1_-1", "5xr1_1", "acc1", "5xl1_0",
    "4bl4", "4xl2", "4xr2", "4bl3", "4bl1", "acc2", "5xl1_3", "3xr2", "dpq", "5x2_-3", "5x2_2", "5br1", "3xl2",
    "5br3", "5xr1_-3", "5x2_-2", "5xl1_4", "5bl3", "5x2_0", "5x2_-1", "5xr1_3", "5x2_1", "5bl4", "5x2_4", "5br4",
    "qit", "5x2_3", "qrot", "co4", "co7", "co3", "co6", "co0", "co5", "co1", "co2", "pr4", "pr2", "pr7", "acc3",
    "dacc", "pr0", "pr5", "pr3", "pr6", "pr1", "fin",
]


def mm(a, b, dims=NN):
    return lax.dot_general(a, b, dims, preferred_element_type=F32)


def iota(shape, dim):
    return lax.broadcasted_iota(jnp.int32, shape, dim)


def split3(v):
    hi = v.astype(BF16)
    rest = v - hi.astype(F32)
    mid = rest.astype(BF16)
    low = (rest - mid.astype(F32)).astype(BF16)
    return hi, mid, low


class Once:
    def __init__(self, copy):
        self.copy, self.done = copy, False

    def wait_recv(self):
        if not self.done:
            self.copy.wait_recv()
            self.done = True


class Gather:
    def __init__(self, buf, slot, sems, sent, pos, at, zr, halves, xr, ways):
        self.slot, self.at, self.sent = slot, at, sent
        self.send, self.recv = sems
        x, z = pos
        fast_z, fast_b, blocks = ways
        z0, zn = zr
        zrow, xrow = pl.ds(z0, zn), pl.ds(*xr)
        h0, h1 = pl.ds(*halves[0]), pl.ds(*halves[1])

        def xm(d):
            return lax.rem(x + d + NX, NX)

        def zm(d):
            return lax.rem(z + d + NZ, NZ)

        plan = {}

        def t(name, to, deps, *where):
            plan[name] = (to, deps, where)

        t("zr1", (0, 1), (), x, z, zrow)
        t("zl1", (0, -1), (), x, z, zrow)
        if fast_z:
            t("zr2", (0, 2), (), x, z, zrow)
            t("zl2", (0, -2), (), x, z, zrow)
            t("zr3", (0, 1), ("zr2",), x, zm(-2), zrow)
            t("zl3", (0, -1), ("zl2",), x, zm(2), zrow)
            t("zr4", (0, 2), ("zr2",), x, zm(-2), h0)
            t("zl4", (0, -2), ("zl2",), x, zm(2), h1)
        else:
            t("zr2", (0, 1), ("zr1",), x, zm(-1), zrow)
            t("zl2", (0, -1), ("zl1",), x, zm(1), zrow)
            t("zr3", (0, 1), ("zr2",), x, zm(-2), zrow)
            t("zl3", (0, -1), ("zl2",), x, zm(2), zrow)
            t("zr4", (0, 1), ("zr3",), x, zm(-3), h0)
            t("zl4", (0, -1), ("zl3",), x, zm(3), h1)
        got_z = tuple(a + i for a in ("zr", "zl") for i in "1234")
        if blocks:
            source = {0: (), -1: ("zr1",), 1: ("zl1",), -2: ("zr2",), 2: ("zl2",), -3: ("zr3",), 3: ("zl3",), 4: ("zr4", "zl4")}
            for d in range(-3, 5):
                t(f"xr1_{d}", (1, 0), source[d], x, zm(d), zrow)
                t(f"xl1_{d}", (-1, 0), source[d], x, zm(d), zrow)
                if d % 2 == 0:
                    t(f"x2_{d}", (1, 0), (f"xr1_{d}",), xm(-1), zm(d), zrow)
                else:
                    t(f"x2_{d}", (-1, 0), (f"xl1_{d}",), xm(1), zm(d), zrow)
        else:
            t("xr1", (1, 0), got_z, x, slice(None), zrow)
            t("xl1", (-1, 0), got_z, x, slice(None), zrow)
            t("xr2", (1, 0), ("xr1",), xm(-1), pl.ds(0, 4), zrow)
            t("xl2", (-1, 0), ("xl1",), xm(1), pl.ds(4, 4), zrow)
        t("axr", (1, 0), (), x, z, xrow)
        t("axl", (-1, 0), (), x, z, xrow)
        t("ax2", (2, 0), (), x, z, xrow)
        got_x = ("axr", "axl", "ax2")
        t("br1", (0, 1), got_x, slice(None), z, xrow)
        t("bl1", (0, -1), got_x, slice(None), z, xrow)
        if fast_b:
            t("br2", (0, 2), got_x, slice(None), z, xrow)
            t("bl2", (0, -2), got_x, slice(None), z, xrow)
            t("br3", (0, 1), ("br2",), slice(None), zm(-2), xrow)
            t("bl3", (0, -1), ("bl2",), slice(None), zm(2), xrow)
            t("br4", (0, 2), ("br2",), pl.ds(0, 2), zm(-2), xrow)
            t("bl4", (0, -2), ("bl2",), pl.ds(2, 2), zm(2), xrow)
        else:
            t("br2", (0, 1), ("br1",), slice(None), zm(-1), xrow)
            t("bl2", (0, -1), ("bl1",), slice(None), zm(1), xrow)
            t("br3", (0, 1), ("br2",), slice(None), zm(-2), xrow)
            t("bl3", (0, -1), ("bl2",), slice(None), zm(2), xrow)
            t("br4", (0, 1), ("br3",), pl.ds(0, 2), zm(-3), xrow)
            t("bl4", (0, -1), ("bl3",), pl.ds(2, 2), zm(3), xrow)
        self.buf, self.plan, self.pos = buf, plan, pos
        self.copies, self.waited = {}, set()

    def run(self, name):
        (dx, dz), deps, where = self.plan[name]
        self.got(deps)
        i = len(self.copies)
        view = self.buf.at[where]
        copy = pltpu.make_async_remote_copy(
            src_ref=view,
            dst_ref=view,
            send_sem=self.send.at[self.slot, i],
            recv_sem=self.recv.at[self.slot, i],
            device_id={"basis": self.at(self.pos[0] + dx, self.pos[1] + dz)},
            device_id_type=MESH,
        )
        copy.start()
        self.copies[name] = copy
        self.sent.append((f"{self.slot + 1}{name}", copy))

    def got(self, names):
        for name in names:
            if name not in self.waited:
                self.copies[name].wait_recv()
                self.waited.add(name)

    def got_all(self):
        self.got(tuple(self.plan))


def kernel(
    og_h, ia_h, rt_h, sq_h, qo_h, qi_h, bo_h, bi_h, eg_h,
    out_ref,
    og, ia, rt, sq, qs, bo, bi, eg,
    qb, ib, tb, rqb, rtb,
    a2s, a2r,
    sel, bisel, inv, hot,
    pinq, pinqr, pint, pintr, pq, pqr, acc, accr,
    qrot, qit, cond, proj, score,
    reds, redr,
    lsem, gsend, grecv, asend, arecv, dsend, drecv, rsend, rrecv,
):
    e = lax.axis_index("expert")
    b = lax.axis_index("basis")
    c = lax.rem(b, NC)
    z = lax.rem(lax.div(b, NC), NZ)
    x = lax.div(b, NC * NZ)

    def at(xx, zz, cc=c):
        return (lax.rem(xx + NX, NX) * NZ + lax.rem(zz + NZ, NZ)) * NC + cc

    sib = {"basis": at(x, z, 1 - c)}
    xc = x * NC + c

    def ypeer(d):
        return {"expert": lax.rem(e + d, NE)}

    def zpeer(d):
        return {"basis": at(x, z + d)}

    def xpeer(d):
        m = lax.rem(xc + d, NX * NC)
        return {"basis": at(lax.div(m, NC), z, lax.rem(m, NC))}

    barrier = pltpu.get_barrier_semaphore()
    for group in (ypeer, zpeer, xpeer):
        for d in range(1, 8):
            pl.semaphore_signal(barrier, inc=1, device_id=group(d), device_id_type=MESH)

    locals_ = [
        (qo_h, qs),
        (qi_h, qb.at[x, z, pl.ds(128, 48)]),
        (rt_h, rt),
        (og_h, og),
        (ia_h, ia),
        (sq_h, sq),
        (bi_h, bi.at[c]),
        (bo_h, bo.at[c]),
        (eg_h, eg.at[c]),
    ]
    local = [pltpu.make_async_copy(s, d, lsem.at[i]) for i, (s, d) in enumerate(locals_)]
    for copy in local:
        copy.start()

    def remote(src, dst, ss, rs, to):
        copy = pltpu.make_async_remote_copy(
            src_ref=src, dst_ref=dst, send_sem=ss, recv_sem=rs, device_id=to, device_id_type=MESH
        )
        copy.start()
        return copy

    to_sib = {}
    sent = []

    def settle(keep=()):
        later = [s for s in sent if s[0].startswith(keep)] if keep else []
        for s in sent:
            if s not in later:
                s[1].wait_send()
        sent[:] = later

    sems = (gsend, grecv)
    pos = (x, z)
    gathers = {
        1: Gather(qb, 0, sems, sent, pos, at, (0, 112), ((0, 64), (64, 48)), (112, 64), WAYS[1]),
        2: Gather(ib, 1, sems, sent, pos, at, (0, 32), ((0, 16), (16, 16)), (32, 16), WAYS[2]),
        3: Gather(tb, 2, sems, sent, pos, at, (0, 192), ((0, 96), (96, 96)), (192, 128), WAYS[3]),
        4: Gather(rqb, 3, sems, sent, pos, at, (0, 32), ((0, 16), (16, 16)), (32, 16), WAYS[4]),
        5: Gather(rtb, 4, sems, sent, pos, at, (0, 32), ((0, 16), (16, 16)), (32, 16), WAYS[5]),
    }
    local[0].wait()
    qb[x, z, 0:128] = qs[...].astype(F32).T.astype(BF16)
    for i in range(1, 6):
        local[i].wait()
    r = rt[...]
    who = iota((8, 128), 0)
    hit = jnp.logical_or(r[0:1, :] == who, r[1:2, :] == who)
    upper = jnp.where(iota((128, 128), 0) < iota((128, 128), 1), 1.0, 0.0).astype(BF16)
    place = mm(jnp.where(hit, 1.0, 0.0).astype(BF16), upper)
    place = jnp.where(hit, place, -1.0).astype(jnp.int32)
    pick = jnp.where(place[:, None, :] == iota((8, CAPP, 128), 1), 1.0, 0.0)
    pick = pick.reshape(8 * CAPP, 128).astype(BF16)
    rows_out = mm(pick, og[...])
    seq_row = jnp.broadcast_to(sq[...], (16, 128)).astype(F32).astype(BF16)
    in_ext = jnp.concatenate([ia[...], seq_row, jnp.zeros((64, 128), BF16)], axis=0)
    rows_in = mm(pick, in_ext, NT)
    a2s[:, :, 0:128] = rows_out.astype(BF16).reshape(8, CAPP, 128)
    a2s[:, :, 128:256] = rows_in.astype(BF16).reshape(8, CAPP, 128)
    a2r[e] = a2s[e]
    w = iota((8, 96, 384), 1) - 48 * c
    want = jnp.logical_and(jnp.logical_and(w >= 0, w < 48), iota((8, 96, 384), 2) == 48 * iota((8, 96, 384), 0) + w)
    sel[...] = jnp.where(want, 1.0, 0.0).reshape(768, 384).astype(BF16)
    pl.semaphore_wait(barrier, 21)

    a2a = []

    def routed_send():
        for d in range(1, 8):
            copy = remote(a2s.at[lax.rem(e + d, NE)], a2r.at[e], asend.at[d - 1], arecv.at[d - 1], ypeer(d))
            a2a.append(copy)
            sent.append((f"a{d}", copy))

    def routed_rows():
        dense = jnp.where(
            iota((8, CAP, 8 * CAPP), 2) == CAPP * iota((8, CAP, 8 * CAPP), 0) + iota((8, CAP, 8 * CAPP), 1), 1.0, 0.0
        ).reshape(8 * CAP, 8 * CAPP)
        dense = jnp.concatenate([dense, jnp.zeros((64, 8 * CAPP), F32)], axis=0).astype(BF16)
        for copy in a2a:
            copy.wait_recv()
        rows = mm(dense, a2r[...].reshape(8 * CAPP, 256))
        tb[x, z] = rows[0:320, 0:128].astype(BF16)
        ib[x, z] = rows[:, 128:256].T[0:48, 0:320].astype(BF16)
        seq_of = rows[0:320, 128 + 48 : 128 + 49]
        hot[...] = jnp.where(seq_of == iota((320, 128), 1).astype(F32), 1.0, 0.0).astype(BF16)

    def pick_in_basis(cc):
        if cc == 0:
            to_sib[0].wait_recv()
            local[6].wait()
        for m in range(4):
            part = mm(bi[cc, :, 768 * m : 768 * (m + 1)], sel[...])
            bisel[48 * cc : 48 * (cc + 1), 384 * m : 384 * (m + 1)] = part.astype(BF16)

    def basis_cols(p):
        cols = pl.ds(pl.multiple_of(256 * p + 128 * c, 128), 128)
        return jnp.concatenate([bo[0, :, cols], bo[1, :, cols]], axis=0)

    def four_cols(p):
        return jnp.concatenate([basis_cols(p + i) for i in range(4)], axis=1)

    def rotate_query_in():
        gathers[1].got_all()
        part = mm(bisel[...], qb[:, :, 128:176, :].reshape(NX * NZ * 48, 128))
        pinq[0] = part[0:48]
        pinq[1] = part[48:96]

    def rotated_query_in():
        to_sib[3].wait_recv()
        rqb[x, z] = (pinq[c] + pinqr[...]).astype(BF16)

    def rotate_query_out(half):
        if half == 0:
            gathers[1].got_all()
            to_sib[1].wait_recv()
            local[7].wait()
            pq[...] = jnp.zeros_like(pq)

        @pl.loop(0, 4)
        def _(i):
            xx, zz = lax.div(i, 2) + 2 * half, 4 * lax.rem(i, 2)
            rhs = jnp.concatenate([qb[xx, zz + k, 0:128, :] for k in range(4)], axis=0)
            pq[...] += mm(four_cols(xx * NZ + zz), rhs)

    def rotated_query_out():
        to_sib[4].wait_recv()
        qrot[...] = (pq[...] + pqr[...]).astype(BF16)

    def invert(i):
        cc, m = lax.div(i, 4), lax.rem(i, 4)
        parts = split3(eg[cc, :, pl.ds(pl.multiple_of(768 * m, 128), 768)])
        chosen = mm(parts[0], sel[...]) + mm(parts[1], sel[...]) + mm(parts[2], sel[...])
        inv[i] = 1.0 / (chosen + damping_shift)

    def turn_queries():
        gathers[4].got_all()
        qit[...] = rqb[...].reshape(NX * NZ * 48, 128).astype(F32).T.astype(BF16)

    def condition(q):
        lane = iota((256, 128), 1)
        mine = jnp.logical_and(lane >= q * QRANK, lane < (q + 1) * QRANK)
        lhs = jnp.where(mine, qrot[...].astype(F32), 0.0).astype(BF16)
        for m in range(4):
            cols = slice(384 * m, 384 * (m + 1))
            gradient = mm(lhs, qit[:, cols])
            for cc in range(2):
                rows = slice(128 * cc, 128 * (cc + 1))
                cond[q, rows, cols] = (gradient[rows] * inv[4 * cc + m]).astype(BF16)

    def rotate_rows_in():
        gathers[2].got_all()
        part = mm(bisel[...], ib[...].reshape(NX * NZ * 48, 320))
        pint[0] = part[0:48]
        pint[1] = part[48:96]

    def rotated_rows_in():
        to_sib[5].wait_recv()
        rtb[x, z] = (pint[c] + pintr[...]).astype(BF16)

    def project(q):
        proj[q] = mm(cond[q], rtb[...].reshape(NX * NZ * 48, 320))

    def rotate_rows_out(part):
        g = gathers[3]
        if part == 0:
            g.got([n for n in g.plan if n[0] in "zab"])
            acc[...] = jnp.zeros_like(acc)
        elif part == 1:
            g.got([n for n in g.plan if n.startswith("xr1")])
        elif part == 2:
            g.got([n for n in g.plan if n.startswith("xl1")])
        else:
            settle(("3xr2", "3xl2", "3x2_"))
            g.got_all()
        xx = lax.rem(x + (0, NX - 1, 1, 2)[part], NX)

        @pl.loop(0, 2)
        def _(i):
            rhs = jnp.concatenate([tb[xx, 4 * i + k] for k in range(4)], axis=1)
            acc[...] += mm(four_cols(xx * NZ + 4 * i), rhs, NT)

    def finish_scores():
        to_sib[6].wait_recv()
        tok = (acc[...] + accr[...]).astype(BF16).astype(F32)
        for q in range(QUERIES):
            score[q : q + 1, :] = jnp.sum(tok * proj[q], axis=0, keepdims=True)

    def sibling(i, src, dst):
        copy = remote(src, dst, dsend.at[i], drecv.at[i], sib)
        to_sib[i] = Once(copy)
        sent.append((f"s{i}", copy))

    tasks = {
        "a2a": routed_send,
        "dbi": lambda: sibling(0, bi_h, bi.at[c]),
        "dbo": lambda: sibling(1, bo_h, bo.at[c]),
        "deg": lambda: sibling(2, eg_h, eg.at[c]),
        "own2": routed_rows,
        "bis0": lambda: pick_in_basis(0),
        "bis1": lambda: pick_in_basis(1),
        "qi": rotate_query_in,
        "dpqi": lambda: sibling(3, pinq.at[1 - c], pinqr),
        "own4": rotated_query_in,
        "qo0": lambda: rotate_query_out(0),
        "qo1": lambda: rotate_query_out(1),
        "dpq": lambda: sibling(4, pq, pqr),
        "qrot": rotated_query_out,
        "qit": turn_queries,
        "rin": rotate_rows_in,
        "drt": lambda: sibling(5, pint.at[1 - c], pintr),
        "own5": rotated_rows_in,
        "acc0": lambda: rotate_rows_out(0),
        "acc1": lambda: rotate_rows_out(1),
        "acc2": lambda: rotate_rows_out(2),
        "acc3": lambda: rotate_rows_out(3),
        "dacc": lambda: sibling(6, acc, accr),
        "fin": finish_scores,
    }
    loops = {"inv": [0, invert], "co": [0, condition], "pr": [0, project]}
    at_once = 0
    while at_once < len(ORDER):
        name = ORDER[at_once]
        at_once += 1
        if name[0].isdigit():
            gathers[int(name[0])].run(name[1:])
            continue
        kind = name.rstrip("01234567")
        if kind not in loops:
            tasks[name]()
            continue
        count = 1
        while at_once < len(ORDER) and ORDER[at_once].rstrip("01234567") == kind:
            at_once += 1
            count += 1
        first, body = loops[kind]
        if kind == "inv" and first == 0:
            to_sib[2].wait_recv()
            local[8].wait()
        if kind == "pr":
            gathers[5].got_all()
        pl.loop(first, first + count)(body)
        loops[kind][0] = first + count

    scale = 1.0 / (8.0 * math.sqrt(FF * D * QRANK))
    parts = split3(score[...] * scale)
    total = mm(parts[0], hot[...]) + mm(parts[1], hot[...]) + mm(parts[2], hot[...])

    for s, group in enumerate((xpeer, zpeer, ypeer)):
        reds[s] = total
        for d in range(1, 8):
            remote(reds.at[s], redr.at[s, d - 1], rsend.at[s], rrecv.at[s], group(d))
        settle()
        seven = pltpu.make_async_remote_copy(
            src_ref=redr.at[s],
            dst_ref=redr.at[s],
            send_sem=rsend.at[s],
            recv_sem=rrecv.at[s],
            device_id=group(1),
            device_id_type=MESH,
        )
        sent.append((f"r{s}", seven))
        seven.wait_recv()
        total = total + jnp.sum(redr[s], axis=0)
    settle()
    lane = iota((8, 128), 1)
    col0 = jnp.sum(jnp.where(lane == 2 * b, total, 0.0), axis=1, keepdims=True)
    col1 = jnp.sum(jnp.where(lane == 2 * b + 1, total, 0.0), axis=1, keepdims=True)
    out_ref[...] = jnp.concatenate([col0, col1], axis=1)


def on_device(out_grads, in_acts, routes, seq_ids, query_out, query_in, out_basis, in_basis, eigvals):
    dma = pltpu.SemaphoreType.DMA
    v = pltpu.VMEM
    return pl.pallas_call(
        kernel,
        out_shape=jax.ShapeDtypeStruct((QUERIES, 2), F32),
        in_specs=[pl.BlockSpec(memory_space=pl.ANY)] * 9,
        out_specs=pl.BlockSpec(memory_space=pltpu.VMEM),
        scratch_shapes=[
            v((128, 128), BF16), v((48, 128), BF16), v((2, 128), jnp.int32), v((1, 128), jnp.int32), v((128, 128), BF16),
            v((2, 128, FF), BF16), v((2, 48, D), BF16), v((2, 128, D), F32),
            v((NX, NZ, 176, 128), BF16), v((NX, NZ, 48, 320), BF16), v((NX, NZ, 320, 128), BF16),
            v((NX, NZ, 48, 128), BF16), v((NX, NZ, 48, 320), BF16),
            v((8, CAPP, 256), BF16), v((8, CAPP, 256), BF16),
            v((768, 384), BF16), v((96, 1536), BF16), v((8, 128, 384), F32), v((320, 128), BF16),
            v((2, 48, 128), F32), v((48, 128), F32), v((2, 48, 320), F32), v((48, 320), F32),
            v((256, 128), F32), v((256, 128), F32), v((256, 320), F32), v((256, 320), F32),
            v((256, 128), BF16), v((128, 1536), BF16), v((QUERIES, 256, 1536), BF16), v((QUERIES, 256, 320), F32),
            v((QUERIES, 320), F32),
            v((3, 8, 128), F32), v((3, 7, 8, 128), F32),
            dma((9,)), dma((5, 43)), dma((5, 43)), dma((7,)), dma((7,)), dma((7,)), dma((7,)), dma((3,)), dma((3,)),
        ],
        compiler_params=pltpu.CompilerParams(
            collective_id=0, has_side_effects=True, vmem_limit_bytes=52 * 1024 * 1024
        ),
    )(
        *(
            pltpu.with_memory_space_constraint(a, pltpu.HBM)
            for a in (
                out_grads, in_acts.T, routes.T, seq_ids.reshape(1, -1), query_out[0], query_in[0].T,
                out_basis[0], in_basis[0], eigvals[0],
            )
        )
    )


def solution(mesh):
    return jax.shard_map(
        on_device,
        mesh=mesh,
        in_specs=(
            P("expert", "basis"),
            P("expert", "basis"),
            P("expert", None),
            P("expert"),
            P("expert", None, "basis"),
            P("expert", None, "basis"),
            P("expert", "basis", None),
            P("expert", "basis", None),
            P("expert", "basis", None),
        ),
        out_specs=P(None, "basis"),
        check_vma=False,
    )
```

```python
import math

import jax
import jax.numpy as jnp
from jax import lax
from jax.experimental import pallas as pl
from jax.experimental.pallas import tpu as pltpu
from jax.sharding import PartitionSpec as P

D = 3072
FF = 8192
QUERIES = 8
QRANK = 16
NX, NZ, NC, NE = 4, 8, 2, 8
CAP = 40
CAPP = 48
damping_shift = 0.1
F32 = jnp.float32
BF16 = jnp.bfloat16
MESH = pl.DeviceIdType.MESH
NN = (((1,), (0,)), ((), ()))
NT = (((1,), (1,)), ((), ()))

(
    ZR1, ZL1, ZR2, ZL2, ZR3, ZL3, ZR4, ZL4, XR1, XL1, XR2, XL2,
    AXR, AXL, AX2, BR1, BL1, BR2, BL2, BR3, BL3, BR4, BL4,
) = range(23)
INVERT, CONDITION, PROJECT = 50, 51, 52

WAYS = {
    1: (True, False, False),
    2: (True, False, False),
    3: (False, False, False),
    4: (True, True, False),
    5: (True, True, True),
}

ORDER = [
    0, 1, 102, 101, 113, 114, 103, 4, 112, 116, 100, 2, 115, 50, 104, 107, 105, 106, 5, 202, 203, 212, 213, 214, 201,
    200, 6, 313, 301, 300, 314, 7, 118, 50, 117, 109, 312, 108, 8, 205, 204, 215, 50, 216, 206, 302, 207, 316, 120,
    303, 119, 50, 208, 315, 209, 218, 50, 217, 3, 305, 304, 111, 110, 219, 122, 50, 121, 220, 210, 318, 211, 317, 306,
    307, 9, 10, 221, 222, 308, 309, 11, 402, 413, 400, 403, 401, 320, 319, 414, 412, 17, 18, 404, 50, 19, 512, 502,
    501, 513, 405, 500, 407, 503, 406, 12, 417, 514, 322, 321, 13, 506, 418, 415, 504, 408, 409, 507, 516, 50, 505,
    517, 543, 553, 421, 518, 551, 541, 539, 550, 554, 419, 20, 549, 545, 540, 542, 21, 552, 422, 411, 410, 420, 416,
    22, 555, 310, 14, 560, 565, 515, 311, 519, 538, 561, 556, 520, 563, 562, 544, 564, 522, 567, 521, 16, 566, 15, 51,
    51, 51, 51, 51, 51, 51, 51, 52, 52, 52, 23, 24, 52, 52, 52, 52, 52, 25,
]


def mm(a, b, dims=NN):
    return lax.dot_general(a, b, dims, preferred_element_type=F32)


def iota(shape, dim):
    return lax.broadcasted_iota(jnp.int32, shape, dim)


def split3(v):
    hi = v.astype(BF16)
    rest = v - hi.astype(F32)
    mid = rest.astype(BF16)
    low = (rest - mid.astype(F32)).astype(BF16)
    return hi, mid, low


class Once:
    def __init__(self, copy):
        self.copy, self.done = copy, False

    def wait_recv(self):
        if not self.done:
            self.copy.wait_recv()
            self.done = True


class Gather:
    def __init__(self, buf, slot, sems, sent, pos, at, zr, halves, xr, ways):
        self.slot, self.at, self.sent = slot, at, sent
        self.send, self.recv = sems
        x, z = pos
        fast_z, fast_b, blocks = ways
        z0, zn = zr
        zrow, xrow = pl.ds(z0, zn), pl.ds(*xr)
        h0, h1 = pl.ds(*halves[0]), pl.ds(*halves[1])

        def xm(d):
            return lax.rem(x + d + NX, NX)

        def zm(d):
            return lax.rem(z + d + NZ, NZ)

        plan = {}

        def t(name, to, deps, *where):
            plan[name] = (to, deps, where)

        t(ZR1, (0, 1), (), x, z, zrow)
        t(ZL1, (0, -1), (), x, z, zrow)
        if fast_z:
            t(ZR2, (0, 2), (), x, z, zrow)
            t(ZL2, (0, -2), (), x, z, zrow)
            t(ZR3, (0, 1), (ZR2,), x, zm(-2), zrow)
            t(ZL3, (0, -1), (ZL2,), x, zm(2), zrow)
            t(ZR4, (0, 2), (ZR2,), x, zm(-2), h0)
            t(ZL4, (0, -2), (ZL2,), x, zm(2), h1)
        else:
            t(ZR2, (0, 1), (ZR1,), x, zm(-1), zrow)
            t(ZL2, (0, -1), (ZL1,), x, zm(1), zrow)
            t(ZR3, (0, 1), (ZR2,), x, zm(-2), zrow)
            t(ZL3, (0, -1), (ZL2,), x, zm(2), zrow)
            t(ZR4, (0, 1), (ZR3,), x, zm(-3), h0)
            t(ZL4, (0, -1), (ZL3,), x, zm(3), h1)
        got_z = tuple(range(ZR1, ZL4 + 1))
        if blocks:
            source = {0: (), -1: (ZR1,), 1: (ZL1,), -2: (ZR2,), 2: (ZL2,), -3: (ZR3,), 3: (ZL3,), 4: (ZR4, ZL4)}
            for d in range(-3, 5):
                t(XR1 + 33 + d, (1, 0), source[d], x, zm(d), zrow)
                t(XL1 + 43 + d, (-1, 0), source[d], x, zm(d), zrow)
                if d % 2 == 0:
                    t(XR2 + 53 + d, (1, 0), (XR1 + 33 + d,), xm(-1), zm(d), zrow)
                else:
                    t(XR2 + 53 + d, (-1, 0), (XL1 + 43 + d,), xm(1), zm(d), zrow)
        else:
            t(XR1, (1, 0), got_z, x, slice(None), zrow)
            t(XL1, (-1, 0), got_z, x, slice(None), zrow)
            t(XR2, (1, 0), (XR1,), xm(-1), pl.ds(0, 4), zrow)
            t(XL2, (-1, 0), (XL1,), xm(1), pl.ds(4, 4), zrow)
        t(AXR, (1, 0), (), x, z, xrow)
        t(AXL, (-1, 0), (), x, z, xrow)
        t(AX2, (2, 0), (), x, z, xrow)
        got_x = (AXR, AXL, AX2)
        t(BR1, (0, 1), got_x, slice(None), z, xrow)
        t(BL1, (0, -1), got_x, slice(None), z, xrow)
        if fast_b:
            t(BR2, (0, 2), got_x, slice(None), z, xrow)
            t(BL2, (0, -2), got_x, slice(None), z, xrow)
            t(BR3, (0, 1), (BR2,), slice(None), zm(-2), xrow)
            t(BL3, (0, -1), (BL2,), slice(None), zm(2), xrow)
            t(BR4, (0, 2), (BR2,), pl.ds(0, 2), zm(-2), xrow)
            t(BL4, (0, -2), (BL2,), pl.ds(2, 2), zm(2), xrow)
        else:
            t(BR2, (0, 1), (BR1,), slice(None), zm(-1), xrow)
            t(BL2, (0, -1), (BL1,), slice(None), zm(1), xrow)
            t(BR3, (0, 1), (BR2,), slice(None), zm(-2), xrow)
            t(BL3, (0, -1), (BL2,), slice(None), zm(2), xrow)
            t(BR4, (0, 1), (BR3,), pl.ds(0, 2), zm(-3), xrow)
            t(BL4, (0, -1), (BL3,), pl.ds(2, 2), zm(3), xrow)
        self.buf, self.plan, self.pos = buf, plan, pos
        self.copies, self.waited = {}, set()

    def run(self, name):
        (dx, dz), deps, where = self.plan[name]
        self.got(deps)
        i = len(self.copies)
        view = self.buf.at[where]
        copy = pltpu.make_async_remote_copy(
            src_ref=view,
            dst_ref=view,
            send_sem=self.send.at[self.slot, i],
            recv_sem=self.recv.at[self.slot, i],
            device_id={"basis": self.at(self.pos[0] + dx, self.pos[1] + dz)},
            device_id_type=MESH,
        )
        copy.start()
        self.copies[name] = copy
        self.sent.append((100 * (self.slot + 1) + name, copy))

    def got(self, names):
        for name in names:
            if name not in self.waited:
                self.copies[name].wait_recv()
                self.waited.add(name)

    def got_all(self):
        self.got(tuple(self.plan))


def kernel(
    og_h, ia_h, rt_h, sq_h, qo_h, qi_h, bo_h, bi_h, eg_h,
    out_ref,
    og, ia, rt, sq, qs, bo, bi, eg,
    qb, ib, tb, rqb, rtb,
    a2s, a2r, a2si, a2ri,
    sel, bisel, inv, hot,
    pinq, pinqr, pint, pintr, pq, pqr, acc, accr,
    qrot, qit, cond, proj, score,
    reds, redr,
    lsem, gsend, grecv, asend, arecv, dsend, drecv, rsend, rrecv,
):
    e = lax.axis_index("expert")
    b = lax.axis_index("basis")
    c = lax.rem(b, NC)
    z = lax.rem(lax.div(b, NC), NZ)
    x = lax.div(b, NC * NZ)

    def at(xx, zz, cc=c):
        return (lax.rem(xx + NX, NX) * NZ + lax.rem(zz + NZ, NZ)) * NC + cc

    sib = {"basis": at(x, z, 1 - c)}
    xc = x * NC + c

    def ypeer(d):
        return {"expert": lax.rem(e + d, NE)}

    def zpeer(d):
        return {"basis": at(x, z + d)}

    def xpeer(d):
        m = lax.rem(xc + d, NX * NC)
        return {"basis": at(lax.div(m, NC), z, lax.rem(m, NC))}

    barrier = pltpu.get_barrier_semaphore()
    for group in (ypeer, zpeer, xpeer):
        for d in range(1, 8):
            pl.semaphore_signal(barrier, inc=1, device_id=group(d), device_id_type=MESH)

    locals_ = [
        (qo_h, qs),
        (qi_h, qb.at[x, z, pl.ds(128, 48)]),
        (rt_h, rt),
        (og_h, og),
        (ia_h, ia),
        (sq_h, sq),
        (bi_h, bi.at[c]),
        (bo_h, bo.at[c]),
        (eg_h, eg.at[c]),
    ]
    local = [pltpu.make_async_copy(s, d, lsem.at[i]) for i, (s, d) in enumerate(locals_)]
    for copy in local:
        copy.start()

    def remote(src, dst, ss, rs, to):
        copy = pltpu.make_async_remote_copy(
            src_ref=src, dst_ref=dst, send_sem=ss, recv_sem=rs, device_id=to, device_id_type=MESH
        )
        copy.start()
        return copy

    to_sib = {}
    sent = []

    def settle(keep=()):
        later = [s for s in sent if s[0] in keep]
        for s in sent:
            if s not in later:
                s[1].wait_send()
        sent[:] = later

    sems = (gsend, grecv)
    pos = (x, z)
    gathers = {
        1: Gather(qb, 0, sems, sent, pos, at, (0, 112), ((0, 64), (64, 48)), (112, 64), WAYS[1]),
        2: Gather(ib, 1, sems, sent, pos, at, (0, 32), ((0, 16), (16, 16)), (32, 16), WAYS[2]),
        3: Gather(tb, 2, sems, sent, pos, at, (0, 192), ((0, 96), (96, 96)), (192, 128), WAYS[3]),
        4: Gather(rqb, 3, sems, sent, pos, at, (0, 32), ((0, 16), (16, 16)), (32, 16), WAYS[4]),
        5: Gather(rtb, 4, sems, sent, pos, at, (0, 32), ((0, 16), (16, 16)), (32, 16), WAYS[5]),
    }
    local[0].wait()
    qb[x, z, 0:128] = qs[...].astype(F32).T.astype(BF16)
    for i in range(1, 6):
        local[i].wait()
    r = rt[...]
    who = iota((8, 128), 0)
    hit = jnp.logical_or(r[0:1, :] == who, r[1:2, :] == who)
    upper = jnp.where(iota((128, 128), 0) < iota((128, 128), 1), 1.0, 0.0).astype(BF16)
    place = mm(jnp.where(hit, 1.0, 0.0).astype(BF16), upper)
    place = jnp.where(hit, place, -1.0).astype(jnp.int32)
    pick = jnp.where(place[:, None, :] == iota((8, CAPP, 128), 1), 1.0, 0.0)
    pick = pick.reshape(8 * CAPP, 128).astype(BF16)
    rows_out = mm(pick, og[...])
    seq_row = jnp.broadcast_to(sq[...], (16, 128)).astype(F32).astype(BF16)
    in_ext = jnp.concatenate([ia[...], seq_row, jnp.zeros((64, 128), BF16)], axis=0)
    rows_in = mm(pick, in_ext, NT)
    a2si[...] = rows_in.astype(BF16).reshape(8, CAPP, 128)
    a2s[...] = rows_out.astype(BF16).reshape(8, CAPP, 128)
    a2ri[e] = a2si[e]
    a2r[e] = a2s[e]
    w = iota((8, 96, 384), 1) - 48 * c
    want = jnp.logical_and(jnp.logical_and(w >= 0, w < 48), iota((8, 96, 384), 2) == 48 * iota((8, 96, 384), 0) + w)
    sel[...] = jnp.where(want, 1.0, 0.0).reshape(768, 384).astype(BF16)
    pl.semaphore_wait(barrier, 21)

    a2a = {}

    def routed_send(src, dst, first):
        a2a[first] = []
        for d in range(1, 8):
            i = first + d - 1
            copy = remote(src.at[lax.rem(e + d, NE)], dst.at[e], asend.at[i], arecv.at[i], ypeer(d))
            a2a[first].append(copy)
            sent.append((0, copy))

    def dense():
        shape = (8, CAP, 8 * CAPP)
        there = jnp.where(iota(shape, 2) == CAPP * iota(shape, 0) + iota(shape, 1), 1.0, 0.0)
        there = there.reshape(8 * CAP, 8 * CAPP)
        return jnp.concatenate([there, jnp.zeros((64, 8 * CAPP), F32)], axis=0).astype(BF16)

    def routed_in():
        for copy in a2a[0]:
            copy.wait_recv()
        rows = mm(dense(), a2ri[...].reshape(8 * CAPP, 128))
        ib[x, z] = rows.T[0:48, 0:320].astype(BF16)
        hot[...] = jnp.where(rows[0:320, 48:49] == iota((320, 128), 1).astype(F32), 1.0, 0.0).astype(BF16)

    def routed_out():
        for copy in a2a[7]:
            copy.wait_recv()
        rows = mm(dense(), a2r[...].reshape(8 * CAPP, 128))
        tb[x, z] = rows[0:320].astype(BF16)

    def pick_in_basis(cc):
        if cc == 0:
            to_sib[0].wait_recv()
            local[6].wait()
        for m in range(4):
            part = mm(bi[cc, :, 768 * m : 768 * (m + 1)], sel[...])
            bisel[48 * cc : 48 * (cc + 1), 384 * m : 384 * (m + 1)] = part.astype(BF16)

    def basis_cols(p):
        cols = pl.ds(pl.multiple_of(256 * p + 128 * c, 128), 128)
        return jnp.concatenate([bo[0, :, cols], bo[1, :, cols]], axis=0)

    def four_cols(p):
        return jnp.concatenate([basis_cols(p + i) for i in range(4)], axis=1)

    def rotate_query_in():
        gathers[1].got_all()
        part = mm(bisel[...], qb[:, :, 128:176, :].reshape(NX * NZ * 48, 128))
        pinq[0] = part[0:48]
        pinq[1] = part[48:96]

    def rotated_query_in():
        to_sib[3].wait_recv()
        rqb[x, z] = (pinq[c] + pinqr[...]).astype(BF16)

    def rotate_query_out(half):
        if half == 0:
            gathers[1].got_all()
            to_sib[1].wait_recv()
            local[7].wait()
            pq[...] = jnp.zeros_like(pq)

        @pl.loop(0, 4)
        def _(i):
            xx, zz = lax.div(i, 2) + 2 * half, 4 * lax.rem(i, 2)
            rhs = jnp.concatenate([qb[xx, zz + k, 0:128, :] for k in range(4)], axis=0)
            pq[...] += mm(four_cols(xx * NZ + zz), rhs)

    def rotated_query_out():
        to_sib[4].wait_recv()
        qrot[...] = (pq[...] + pqr[...]).astype(BF16)

    def invert(i):
        cc, m = lax.div(i, 4), lax.rem(i, 4)
        parts = split3(eg[cc, :, pl.ds(pl.multiple_of(768 * m, 128), 768)])
        chosen = mm(parts[0], sel[...]) + mm(parts[1], sel[...]) + mm(parts[2], sel[...])
        inv[i] = 1.0 / (chosen + damping_shift)

    def turn_queries():
        gathers[4].got_all()
        qit[...] = rqb[...].reshape(NX * NZ * 48, 128).astype(F32).T.astype(BF16)

    def condition(q):
        lane = iota((256, 128), 1)
        mine = jnp.logical_and(lane >= q * QRANK, lane < (q + 1) * QRANK)
        lhs = jnp.where(mine, qrot[...].astype(F32), 0.0).astype(BF16)
        for m in range(4):
            cols = slice(384 * m, 384 * (m + 1))
            gradient = mm(lhs, qit[:, cols])
            for cc in range(2):
                rows = slice(128 * cc, 128 * (cc + 1))
                cond[q, rows, cols] = (gradient[rows] * inv[4 * cc + m]).astype(BF16)

    def rotate_rows_in():
        gathers[2].got_all()
        part = mm(bisel[...], ib[...].reshape(NX * NZ * 48, 320))
        pint[0] = part[0:48]
        pint[1] = part[48:96]

    def rotated_rows_in():
        to_sib[5].wait_recv()
        rtb[x, z] = (pint[c] + pintr[...]).astype(BF16)

    def project(q):
        proj[q] = mm(cond[q], rtb[...].reshape(NX * NZ * 48, 320))

    def rotate_rows_out(part):
        g = gathers[3]
        if part == 0:
            g.got([n for n in g.plan if n < XR1 or AXR <= n <= BL4])
            acc[...] = jnp.zeros_like(acc)
        elif part == 1:
            g.got([n for n in g.plan if n == XR1 or XR1 + 30 <= n < XR1 + 38])
        elif part == 2:
            g.got([n for n in g.plan if n == XL1 or XL1 + 40 <= n < XL1 + 48])
        else:
            settle([300 + XR2, 300 + XL2] + list(range(300 + XR2 + 50, 300 + XR2 + 58)))
            g.got_all()
        xx = lax.rem(x + (0, NX - 1, 1, 2)[part], NX)

        @pl.loop(0, 2)
        def _(i):
            rhs = jnp.concatenate([tb[xx, 4 * i + k] for k in range(4)], axis=1)
            acc[...] += mm(four_cols(xx * NZ + 4 * i), rhs, NT)

    def finish_scores():
        to_sib[6].wait_recv()
        tok = (acc[...] + accr[...]).astype(BF16).astype(F32)
        for q in range(QUERIES):
            score[q : q + 1, :] = jnp.sum(tok * proj[q], axis=0, keepdims=True)

    def sibling(i, src, dst):
        copy = remote(src, dst, dsend.at[i], drecv.at[i], sib)
        to_sib[i] = Once(copy)
        sent.append((0, copy))

    tasks = [
        lambda: routed_send(a2si, a2ri, 0),
        lambda: routed_send(a2s, a2r, 7),
        lambda: sibling(0, bi_h, bi.at[c]),
        lambda: sibling(1, bo_h, bo.at[c]),
        lambda: sibling(2, eg_h, eg.at[c]),
        routed_in,
        routed_out,
        lambda: pick_in_basis(0),
        lambda: pick_in_basis(1),
        rotate_query_in,
        lambda: sibling(3, pinq.at[1 - c], pinqr),
        rotated_query_in,
        lambda: rotate_query_out(0),
        lambda: rotate_query_out(1),
        lambda: sibling(4, pq, pqr),
        rotated_query_out,
        turn_queries,
        rotate_rows_in,
        lambda: sibling(5, pint.at[1 - c], pintr),
        rotated_rows_in,
        lambda: rotate_rows_out(0),
        lambda: rotate_rows_out(1),
        lambda: rotate_rows_out(2),
        lambda: rotate_rows_out(3),
        lambda: sibling(6, acc, accr),
        finish_scores,
    ]
    loops = {INVERT: [0, invert], CONDITION: [0, condition], PROJECT: [0, project]}
    step = 0
    while step < len(ORDER):
        code = ORDER[step]
        step += 1
        if code >= 100:
            gathers[code // 100].run(code % 100)
            continue
        if code not in loops:
            tasks[code]()
            continue
        count = 1
        while step < len(ORDER) and ORDER[step] == code:
            step += 1
            count += 1
        first, body = loops[code]
        if code == INVERT and first == 0:
            to_sib[2].wait_recv()
            local[8].wait()
        if code == PROJECT:
            gathers[5].got_all()
        pl.loop(first, first + count)(body)
        loops[code][0] = first + count

    scale = 1.0 / (8.0 * math.sqrt(FF * D * QRANK))
    parts = split3(score[...] * scale)
    total = mm(parts[0], hot[...]) + mm(parts[1], hot[...]) + mm(parts[2], hot[...])

    for s, group in enumerate((xpeer, zpeer, ypeer)):
        reds[s] = total
        for d in range(1, 8):
            remote(reds.at[s], redr.at[s, d - 1], rsend.at[s], rrecv.at[s], group(d))
        settle()
        seven = pltpu.make_async_remote_copy(
            src_ref=redr.at[s],
            dst_ref=redr.at[s],
            send_sem=rsend.at[s],
            recv_sem=rrecv.at[s],
            device_id=group(1),
            device_id_type=MESH,
        )
        sent.append((0, seven))
        seven.wait_recv()
        total = total + jnp.sum(redr[s], axis=0)
    settle()
    lane = iota((8, 128), 1)
    col0 = jnp.sum(jnp.where(lane == 2 * b, total, 0.0), axis=1, keepdims=True)
    col1 = jnp.sum(jnp.where(lane == 2 * b + 1, total, 0.0), axis=1, keepdims=True)
    out_ref[...] = jnp.concatenate([col0, col1], axis=1)


def on_device(out_grads, in_acts, routes, seq_ids, query_out, query_in, out_basis, in_basis, eigvals):
    dma = pltpu.SemaphoreType.DMA
    v = pltpu.VMEM
    return pl.pallas_call(
        kernel,
        out_shape=jax.ShapeDtypeStruct((QUERIES, 2), F32),
        in_specs=[pl.BlockSpec(memory_space=pl.ANY)] * 9,
        out_specs=pl.BlockSpec(memory_space=pltpu.VMEM),
        scratch_shapes=[
            v((128, 128), BF16), v((48, 128), BF16), v((2, 128), jnp.int32), v((1, 128), jnp.int32), v((128, 128), BF16),
            v((2, 128, FF), BF16), v((2, 48, D), BF16), v((2, 128, D), F32),
            v((NX, NZ, 176, 128), BF16), v((NX, NZ, 48, 320), BF16), v((NX, NZ, 320, 128), BF16),
            v((NX, NZ, 48, 128), BF16), v((NX, NZ, 48, 320), BF16),
            v((8, CAPP, 128), BF16), v((8, CAPP, 128), BF16), v((8, CAPP, 128), BF16), v((8, CAPP, 128), BF16),
            v((768, 384), BF16), v((96, 1536), BF16), v((8, 128, 384), F32), v((320, 128), BF16),
            v((2, 48, 128), F32), v((48, 128), F32), v((2, 48, 320), F32), v((48, 320), F32),
            v((256, 128), F32), v((256, 128), F32), v((256, 320), F32), v((256, 320), F32),
            v((256, 128), BF16), v((128, 1536), BF16), v((QUERIES, 256, 1536), BF16), v((QUERIES, 256, 320), F32),
            v((QUERIES, 320), F32),
            v((3, 8, 128), F32), v((3, 7, 8, 128), F32),
            dma((9,)), dma((5, 43)), dma((5, 43)), dma((14,)), dma((14,)), dma((7,)), dma((7,)), dma((3,)), dma((3,)),
        ],
        compiler_params=pltpu.CompilerParams(
            collective_id=0, has_side_effects=True, vmem_limit_bytes=52 * 1024 * 1024
        ),
    )(
        *(
            pltpu.with_memory_space_constraint(a, pltpu.HBM)
            for a in (
                out_grads, in_acts.T, routes.T, seq_ids.reshape(1, -1), query_out[0], query_in[0].T,
                out_basis[0], in_basis[0], eigvals[0],
            )
        )
    )


def solution(mesh):
    return jax.shard_map(
        on_device,
        mesh=mesh,
        in_specs=(
            P("expert", "basis"),
            P("expert", "basis"),
            P("expert", None),
            P("expert"),
            P("expert", None, "basis"),
            P("expert", None, "basis"),
            P("expert", "basis", None),
            P("expert", "basis", None),
            P("expert", "basis", None),
        ),
        out_specs=P(None, "basis"),
        check_vma=False,
    )
```

```python
import math

import jax
import jax.numpy as jnp
from jax import lax
from jax.experimental import pallas as pl
from jax.experimental.pallas import tpu as pltpu
from jax.sharding import PartitionSpec as P

D = 3072
FF = 8192
QUERIES = 8
QRANK = 16
NX, NZ, NC, NE = 4, 8, 2, 8
CAP = 40
CAPP = 48
damping_shift = 0.1
F32 = jnp.float32
BF16 = jnp.bfloat16
MESH = pl.DeviceIdType.MESH
NN = (((1,), (0,)), ((), ()))
NT = (((1,), (1,)), ((), ()))

(
    ZR1, ZL1, ZR2, ZL2, ZR3, ZL3, ZR4, ZL4, XR1, XL1, XR2, XL2,
    AXR, AXL, AX2, BR1, BL1, BR2, BL2, BR3, BL3, BR4, BL4,
) = range(23)
INVERT, CONDITION, PROJECT = 50, 51, 52

WAYS = {
    1: (True, False, False),
    2: (True, True, False),
    3: (False, False, True),
    4: (True, True, False),
    5: (True, True, True),
}

ORDER = [
    0, 114, 4, 102, 103, 101, 113, 1, 112, 106, 115, 116, 104, 2, 105, 100, 107, 5, 212, 6, 314, 201, 203, 301, 341,
    214, 313, 3, 300, 109, 202, 213, 108, 7, 118, 352, 117, 312, 200, 205, 207, 303, 302, 206, 216, 204, 50, 351, 342,
    218, 119, 217, 315, 209, 208, 120, 316, 220, 111, 110, 219, 121, 50, 122, 8, 50, 317, 305, 221, 50, 350, 50, 211,
    353, 340, 354, 210, 343, 50, 318, 304, 363, 222, 9, 10, 12, 11, 414, 402, 215, 403, 413, 412, 13, 339, 306, 50,
    401, 400, 50, 344, 406, 349, 417, 405, 404, 407, 418, 320, 362, 14, 319, 338, 307, 17, 355, 408, 18, 360, 15, 19,
    502, 514, 501, 512, 361, 500, 513, 503, 345, 409, 321, 421, 322, 366, 552, 553, 410, 356, 504, 505, 365, 517, 550,
    539, 422, 543, 507, 518, 506, 411, 420, 419, 416, 415, 515, 554, 542, 541, 20, 538, 555, 551, 21, 544, 549, 545,
    565, 556, 364, 516, 561, 540, 564, 563, 367, 22, 522, 520, 521, 16, 562, 51, 519, 51, 566, 51, 567, 560, 51, 51,
    51, 51, 23, 52, 52, 52, 52, 24, 52, 51, 52, 52, 52, 25,
]


def mm(a, b, dims=NN):
    return lax.dot_general(a, b, dims, preferred_element_type=F32)


def iota(shape, dim):
    return lax.broadcasted_iota(jnp.int32, shape, dim)


def split3(v):
    hi = v.astype(BF16)
    rest = v - hi.astype(F32)
    mid = rest.astype(BF16)
    low = (rest - mid.astype(F32)).astype(BF16)
    return hi, mid, low


class Once:
    def __init__(self, copy):
        self.copy, self.done = copy, False

    def wait_recv(self):
        if not self.done:
            self.copy.wait_recv()
            self.done = True


class Gather:
    def __init__(self, buf, slot, sems, sent, pos, at, zr, halves, xr, ways):
        self.slot, self.at, self.sent = slot, at, sent
        self.send, self.recv = sems
        x, z = pos
        fast_z, fast_b, blocks = ways
        z0, zn = zr
        zrow, xrow = pl.ds(z0, zn), pl.ds(*xr)
        h0, h1 = pl.ds(*halves[0]), pl.ds(*halves[1])

        def xm(d):
            return lax.rem(x + d + NX, NX)

        def zm(d):
            return lax.rem(z + d + NZ, NZ)

        plan = {}

        def t(name, to, deps, *where):
            plan[name] = (to, deps, where)

        t(ZR1, (0, 1), (), x, z, zrow)
        t(ZL1, (0, -1), (), x, z, zrow)
        if fast_z:
            t(ZR2, (0, 2), (), x, z, zrow)
            t(ZL2, (0, -2), (), x, z, zrow)
            t(ZR3, (0, 1), (ZR2,), x, zm(-2), zrow)
            t(ZL3, (0, -1), (ZL2,), x, zm(2), zrow)
            t(ZR4, (0, 2), (ZR2,), x, zm(-2), h0)
            t(ZL4, (0, -2), (ZL2,), x, zm(2), h1)
        else:
            t(ZR2, (0, 1), (ZR1,), x, zm(-1), zrow)
            t(ZL2, (0, -1), (ZL1,), x, zm(1), zrow)
            t(ZR3, (0, 1), (ZR2,), x, zm(-2), zrow)
            t(ZL3, (0, -1), (ZL2,), x, zm(2), zrow)
            t(ZR4, (0, 1), (ZR3,), x, zm(-3), h0)
            t(ZL4, (0, -1), (ZL3,), x, zm(3), h1)
        got_z = tuple(range(ZR1, ZL4 + 1))
        if blocks:
            source = {0: (), -1: (ZR1,), 1: (ZL1,), -2: (ZR2,), 2: (ZL2,), -3: (ZR3,), 3: (ZL3,), 4: (ZR4, ZL4)}
            for d in range(-3, 5):
                t(XR1 + 33 + d, (1, 0), source[d], x, zm(d), zrow)
                t(XL1 + 43 + d, (-1, 0), source[d], x, zm(d), zrow)
                if d % 2 == 0:
                    t(XR2 + 53 + d, (1, 0), (XR1 + 33 + d,), xm(-1), zm(d), zrow)
                else:
                    t(XR2 + 53 + d, (-1, 0), (XL1 + 43 + d,), xm(1), zm(d), zrow)
        else:
            t(XR1, (1, 0), got_z, x, slice(None), zrow)
            t(XL1, (-1, 0), got_z, x, slice(None), zrow)
            t(XR2, (1, 0), (XR1,), xm(-1), pl.ds(0, 4), zrow)
            t(XL2, (-1, 0), (XL1,), xm(1), pl.ds(4, 4), zrow)
        t(AXR, (1, 0), (), x, z, xrow)
        t(AXL, (-1, 0), (), x, z, xrow)
        t(AX2, (2, 0), (), x, z, xrow)
        got_x = (AXR, AXL, AX2)
        t(BR1, (0, 1), got_x, slice(None), z, xrow)
        t(BL1, (0, -1), got_x, slice(None), z, xrow)
        if fast_b:
            t(BR2, (0, 2), got_x, slice(None), z, xrow)
            t(BL2, (0, -2), got_x, slice(None), z, xrow)
            t(BR3, (0, 1), (BR2,), slice(None), zm(-2), xrow)
            t(BL3, (0, -1), (BL2,), slice(None), zm(2), xrow)
            t(BR4, (0, 2), (BR2,), pl.ds(0, 2), zm(-2), xrow)
            t(BL4, (0, -2), (BL2,), pl.ds(2, 2), zm(2), xrow)
        else:
            t(BR2, (0, 1), (BR1,), slice(None), zm(-1), xrow)
            t(BL2, (0, -1), (BL1,), slice(None), zm(1), xrow)
            t(BR3, (0, 1), (BR2,), slice(None), zm(-2), xrow)
            t(BL3, (0, -1), (BL2,), slice(None), zm(2), xrow)
            t(BR4, (0, 1), (BR3,), pl.ds(0, 2), zm(-3), xrow)
            t(BL4, (0, -1), (BL3,), pl.ds(2, 2), zm(3), xrow)
        self.buf, self.plan, self.pos = buf, plan, pos
        self.copies, self.waited = {}, set()

    def run(self, name):
        (dx, dz), deps, where = self.plan[name]
        self.got(deps)
        i = len(self.copies)
        view = self.buf.at[where]
        copy = pltpu.make_async_remote_copy(
            src_ref=view,
            dst_ref=view,
            send_sem=self.send.at[self.slot, i],
            recv_sem=self.recv.at[self.slot, i],
            device_id={"basis": self.at(self.pos[0] + dx, self.pos[1] + dz)},
            device_id_type=MESH,
        )
        copy.start()
        self.copies[name] = copy
        self.sent.append((100 * (self.slot + 1) + name, copy))

    def got(self, names):
        for name in names:
            if name not in self.waited:
                self.copies[name].wait_recv()
                self.waited.add(name)

    def got_all(self):
        self.got(tuple(self.plan))


def kernel(
    og_h, ia_h, rt_h, sq_h, qo_h, qi_h, bo_h, bi_h, eg_h,
    out_ref,
    og, ia, rt, sq, qs, bo, bi, eg,
    qb, ib, tb, rqb, rtb,
    a2s, a2r, a2si, a2ri,
    sel, bisel, inv, hot,
    pinq, pinqr, pint, pintr, pq, pqr, acc, accr,
    qrot, qit, cond, proj, score,
    reds, redr,
    lsem, gsend, grecv, asend, arecv, dsend, drecv, rsend, rrecv,
):
    e = lax.axis_index("expert")
    b = lax.axis_index("basis")
    c = lax.rem(b, NC)
    z = lax.rem(lax.div(b, NC), NZ)
    x = lax.div(b, NC * NZ)

    def at(xx, zz, cc=c):
        return (lax.rem(xx + NX, NX) * NZ + lax.rem(zz + NZ, NZ)) * NC + cc

    sib = {"basis": at(x, z, 1 - c)}
    xc = x * NC + c

    def ypeer(d):
        return {"expert": lax.rem(e + d, NE)}

    def zpeer(d):
        return {"basis": at(x, z + d)}

    def xpeer(d):
        m = lax.rem(xc + d, NX * NC)
        return {"basis": at(lax.div(m, NC), z, lax.rem(m, NC))}

    barrier = pltpu.get_barrier_semaphore()
    for group in (ypeer, zpeer, xpeer):
        for d in range(1, 8):
            pl.semaphore_signal(barrier, inc=1, device_id=group(d), device_id_type=MESH)

    locals_ = [
        (qo_h, qs),
        (qi_h, qb.at[x, z, pl.ds(128, 48)]),
        (rt_h, rt),
        (og_h, og),
        (ia_h, ia),
        (sq_h, sq),
        (bi_h, bi.at[c]),
        (bo_h, bo.at[c]),
        (eg_h, eg.at[c]),
    ]
    local = [pltpu.make_async_copy(s, d, lsem.at[i]) for i, (s, d) in enumerate(locals_)]
    for copy in local:
        copy.start()

    def remote(src, dst, ss, rs, to):
        copy = pltpu.make_async_remote_copy(
            src_ref=src, dst_ref=dst, send_sem=ss, recv_sem=rs, device_id=to, device_id_type=MESH
        )
        copy.start()
        return copy

    to_sib = {}
    sent = []

    def settle(keep=()):
        later = [s for s in sent if s[0] in keep]
        for s in sent:
            if s not in later:
                s[1].wait_send()
        sent[:] = later

    sems = (gsend, grecv)
    pos = (x, z)
    gathers = {
        1: Gather(qb, 0, sems, sent, pos, at, (0, 112), ((0, 64), (64, 48)), (112, 64), WAYS[1]),
        2: Gather(ib, 1, sems, sent, pos, at, (0, 32), ((0, 16), (16, 16)), (32, 16), WAYS[2]),
        3: Gather(tb, 2, sems, sent, pos, at, (0, 192), ((0, 96), (96, 96)), (192, 128), WAYS[3]),
        4: Gather(rqb, 3, sems, sent, pos, at, (0, 32), ((0, 16), (16, 16)), (32, 16), WAYS[4]),
        5: Gather(rtb, 4, sems, sent, pos, at, (0, 32), ((0, 16), (16, 16)), (32, 16), WAYS[5]),
    }
    local[0].wait()
    qb[x, z, 0:128] = qs[...].astype(F32).T.astype(BF16)
    for i in range(1, 6):
        local[i].wait()
    r = rt[...]
    who = iota((8, 128), 0)
    hit = jnp.logical_or(r[0:1, :] == who, r[1:2, :] == who)
    upper = jnp.where(iota((128, 128), 0) < iota((128, 128), 1), 1.0, 0.0).astype(BF16)
    place = mm(jnp.where(hit, 1.0, 0.0).astype(BF16), upper)
    place = jnp.where(hit, place, -1.0).astype(jnp.int32)
    pick = jnp.where(place[:, None, :] == iota((8, CAPP, 128), 1), 1.0, 0.0)
    pick = pick.reshape(8 * CAPP, 128).astype(BF16)
    rows_out = mm(pick, og[...])
    seq_row = jnp.broadcast_to(sq[...], (16, 128)).astype(F32).astype(BF16)
    in_ext = jnp.concatenate([ia[...], seq_row, jnp.zeros((64, 128), BF16)], axis=0)
    rows_in = mm(pick, in_ext, NT)
    a2si[...] = rows_in.astype(BF16).reshape(8, CAPP, 128)
    a2s[...] = rows_out.astype(BF16).reshape(8, CAPP, 128)
    a2ri[e] = a2si[e]
    a2r[e] = a2s[e]
    w = iota((8, 96, 384), 1) - 48 * c
    want = jnp.logical_and(jnp.logical_and(w >= 0, w < 48), iota((8, 96, 384), 2) == 48 * iota((8, 96, 384), 0) + w)
    sel[...] = jnp.where(want, 1.0, 0.0).reshape(768, 384).astype(BF16)
    pl.semaphore_wait(barrier, 21)

    a2a = {}

    def routed_send(src, dst, first):
        a2a[first] = []
        for d in range(1, 8):
            i = first + d - 1
            copy = remote(src.at[lax.rem(e + d, NE)], dst.at[e], asend.at[i], arecv.at[i], ypeer(d))
            a2a[first].append(copy)
            sent.append((0, copy))

    def dense():
        shape = (8, CAP, 8 * CAPP)
        there = jnp.where(iota(shape, 2) == CAPP * iota(shape, 0) + iota(shape, 1), 1.0, 0.0)
        there = there.reshape(8 * CAP, 8 * CAPP)
        return jnp.concatenate([there, jnp.zeros((64, 8 * CAPP), F32)], axis=0).astype(BF16)

    def routed_in():
        for copy in a2a[0]:
            copy.wait_recv()
        rows = mm(dense(), a2ri[...].reshape(8 * CAPP, 128))
        ib[x, z] = rows.T[0:48, 0:320].astype(BF16)
        hot[...] = jnp.where(rows[0:320, 48:49] == iota((320, 128), 1).astype(F32), 1.0, 0.0).astype(BF16)

    def routed_out():
        for copy in a2a[7]:
            copy.wait_recv()
        rows = mm(dense(), a2r[...].reshape(8 * CAPP, 128))
        tb[x, z] = rows[0:320].astype(BF16)

    def pick_in_basis(cc):
        if cc == 0:
            to_sib[0].wait_recv()
            local[6].wait()
        for m in range(4):
            part = mm(bi[cc, :, 768 * m : 768 * (m + 1)], sel[...])
            bisel[48 * cc : 48 * (cc + 1), 384 * m : 384 * (m + 1)] = part.astype(BF16)

    def basis_cols(p):
        cols = pl.ds(pl.multiple_of(256 * p + 128 * c, 128), 128)
        return jnp.concatenate([bo[0, :, cols], bo[1, :, cols]], axis=0)

    def four_cols(p):
        return jnp.concatenate([basis_cols(p + i) for i in range(4)], axis=1)

    def rotate_query_in():
        gathers[1].got_all()
        part = mm(bisel[...], qb[:, :, 128:176, :].reshape(NX * NZ * 48, 128))
        pinq[0] = part[0:48]
        pinq[1] = part[48:96]

    def rotated_query_in():
        to_sib[3].wait_recv()
        rqb[x, z] = (pinq[c] + pinqr[...]).astype(BF16)

    def rotate_query_out(half):
        if half == 0:
            gathers[1].got_all()
            to_sib[1].wait_recv()
            local[7].wait()
            pq[...] = jnp.zeros_like(pq)

        @pl.loop(0, 4)
        def _(i):
            xx, zz = lax.div(i, 2) + 2 * half, 4 * lax.rem(i, 2)
            rhs = jnp.concatenate([qb[xx, zz + k, 0:128, :] for k in range(4)], axis=0)
            pq[...] += mm(four_cols(xx * NZ + zz), rhs)

    def rotated_query_out():
        to_sib[4].wait_recv()
        qrot[...] = (pq[...] + pqr[...]).astype(BF16)

    def invert(i):
        cc, m = lax.div(i, 4), lax.rem(i, 4)
        parts = split3(eg[cc, :, pl.ds(pl.multiple_of(768 * m, 128), 768)])
        chosen = mm(parts[0], sel[...]) + mm(parts[1], sel[...]) + mm(parts[2], sel[...])
        inv[i] = 1.0 / (chosen + damping_shift)

    def turn_queries():
        gathers[4].got_all()
        qit[...] = rqb[...].reshape(NX * NZ * 48, 128).astype(F32).T.astype(BF16)

    def condition(q):
        lane = iota((256, 128), 1)
        mine = jnp.logical_and(lane >= q * QRANK, lane < (q + 1) * QRANK)
        lhs = jnp.where(mine, qrot[...].astype(F32), 0.0).astype(BF16)
        for m in range(4):
            cols = slice(384 * m, 384 * (m + 1))
            gradient = mm(lhs, qit[:, cols])
            for cc in range(2):
                rows = slice(128 * cc, 128 * (cc + 1))
                cond[q, rows, cols] = (gradient[rows] * inv[4 * cc + m]).astype(BF16)

    def rotate_rows_in():
        gathers[2].got_all()
        part = mm(bisel[...], ib[...].reshape(NX * NZ * 48, 320))
        pint[0] = part[0:48]
        pint[1] = part[48:96]

    def rotated_rows_in():
        to_sib[5].wait_recv()
        rtb[x, z] = (pint[c] + pintr[...]).astype(BF16)

    def project(q):
        proj[q] = mm(cond[q], rtb[...].reshape(NX * NZ * 48, 320))

    def rotate_rows_out(part):
        g = gathers[3]
        if part == 0:
            g.got([n for n in g.plan if n < XR1 or AXR <= n <= BL4])
            acc[...] = jnp.zeros_like(acc)
        elif part == 1:
            g.got([n for n in g.plan if n == XR1 or XR1 + 30 <= n < XR1 + 38])
        elif part == 2:
            g.got([n for n in g.plan if n == XL1 or XL1 + 40 <= n < XL1 + 48])
        else:
            settle([300 + XR2, 300 + XL2] + list(range(300 + XR2 + 50, 300 + XR2 + 58)))
            g.got_all()
        xx = lax.rem(x + (0, NX - 1, 1, 2)[part], NX)

        @pl.loop(0, 2)
        def _(i):
            rhs = jnp.concatenate([tb[xx, 4 * i + k] for k in range(4)], axis=1)
            acc[...] += mm(four_cols(xx * NZ + 4 * i), rhs, NT)

    def finish_scores():
        to_sib[6].wait_recv()
        tok = (acc[...] + accr[...]).astype(BF16).astype(F32)
        for q in range(QUERIES):
            score[q : q + 1, :] = jnp.sum(tok * proj[q], axis=0, keepdims=True)

    def sibling(i, src, dst):
        copy = remote(src, dst, dsend.at[i], drecv.at[i], sib)
        to_sib[i] = Once(copy)
        sent.append((0, copy))

    tasks = [
        lambda: routed_send(a2si, a2ri, 0),
        lambda: routed_send(a2s, a2r, 7),
        lambda: sibling(0, bi_h, bi.at[c]),
        lambda: sibling(1, bo_h, bo.at[c]),
        lambda: sibling(2, eg_h, eg.at[c]),
        routed_in,
        routed_out,
        lambda: pick_in_basis(0),
        lambda: pick_in_basis(1),
        rotate_query_in,
        lambda: sibling(3, pinq.at[1 - c], pinqr),
        rotated_query_in,
        lambda: rotate_query_out(0),
        lambda: rotate_query_out(1),
        lambda: sibling(4, pq, pqr),
        rotated_query_out,
        turn_queries,
        rotate_rows_in,
        lambda: sibling(5, pint.at[1 - c], pintr),
        rotated_rows_in,
        lambda: rotate_rows_out(0),
        lambda: rotate_rows_out(1),
        lambda: rotate_rows_out(2),
        lambda: rotate_rows_out(3),
        lambda: sibling(6, acc, accr),
        finish_scores,
    ]
    loops = {INVERT: [0, invert], CONDITION: [0, condition], PROJECT: [0, project]}
    step = 0
    while step < len(ORDER):
        code = ORDER[step]
        step += 1
        if code >= 100:
            gathers[code // 100].run(code % 100)
            continue
        if code not in loops:
            tasks[code]()
            continue
        count = 1
        while step < len(ORDER) and ORDER[step] == code:
            step += 1
            count += 1
        first, body = loops[code]
        if code == INVERT and first == 0:
            to_sib[2].wait_recv()
            local[8].wait()
        if code == PROJECT:
            gathers[5].got_all()
        pl.loop(first, first + count)(body)
        loops[code][0] = first + count

    scale = 1.0 / (8.0 * math.sqrt(FF * D * QRANK))
    parts = split3(score[...] * scale)
    total = mm(parts[0], hot[...]) + mm(parts[1], hot[...]) + mm(parts[2], hot[...])

    for s, group in enumerate((xpeer, zpeer, ypeer)):
        reds[s] = total
        for d in range(1, 8):
            remote(reds.at[s], redr.at[s, d - 1], rsend.at[s], rrecv.at[s], group(d))
        settle()
        seven = pltpu.make_async_remote_copy(
            src_ref=redr.at[s],
            dst_ref=redr.at[s],
            send_sem=rsend.at[s],
            recv_sem=rrecv.at[s],
            device_id=group(1),
            device_id_type=MESH,
        )
        sent.append((0, seven))
        seven.wait_recv()
        total = total + jnp.sum(redr[s], axis=0)
    settle()
    lane = iota((8, 128), 1)
    col0 = jnp.sum(jnp.where(lane == 2 * b, total, 0.0), axis=1, keepdims=True)
    col1 = jnp.sum(jnp.where(lane == 2 * b + 1, total, 0.0), axis=1, keepdims=True)
    out_ref[...] = jnp.concatenate([col0, col1], axis=1)


def on_device(out_grads, in_acts, routes, seq_ids, query_out, query_in, out_basis, in_basis, eigvals):
    dma = pltpu.SemaphoreType.DMA
    v = pltpu.VMEM
    return pl.pallas_call(
        kernel,
        out_shape=jax.ShapeDtypeStruct((QUERIES, 2), F32),
        in_specs=[pl.BlockSpec(memory_space=pl.ANY)] * 9,
        out_specs=pl.BlockSpec(memory_space=pltpu.VMEM),
        scratch_shapes=[
            v((128, 128), BF16), v((48, 128), BF16), v((2, 128), jnp.int32), v((1, 128), jnp.int32), v((128, 128), BF16),
            v((2, 128, FF), BF16), v((2, 48, D), BF16), v((2, 128, D), F32),
            v((NX, NZ, 176, 128), BF16), v((NX, NZ, 48, 320), BF16), v((NX, NZ, 320, 128), BF16),
            v((NX, NZ, 48, 128), BF16), v((NX, NZ, 48, 320), BF16),
            v((8, CAPP, 128), BF16), v((8, CAPP, 128), BF16), v((8, CAPP, 128), BF16), v((8, CAPP, 128), BF16),
            v((768, 384), BF16), v((96, 1536), BF16), v((8, 128, 384), F32), v((320, 128), BF16),
            v((2, 48, 128), F32), v((48, 128), F32), v((2, 48, 320), F32), v((48, 320), F32),
            v((256, 128), F32), v((256, 128), F32), v((256, 320), F32), v((256, 320), F32),
            v((256, 128), BF16), v((128, 1536), BF16), v((QUERIES, 256, 1536), BF16), v((QUERIES, 256, 320), F32),
            v((QUERIES, 320), F32),
            v((3, 8, 128), F32), v((3, 7, 8, 128), F32),
            dma((9,)), dma((5, 43)), dma((5, 43)), dma((14,)), dma((14,)), dma((7,)), dma((7,)), dma((3,)), dma((3,)),
        ],
        compiler_params=pltpu.CompilerParams(
            collective_id=0, has_side_effects=True, vmem_limit_bytes=52 * 1024 * 1024
        ),
    )(
        *(
            pltpu.with_memory_space_constraint(a, pltpu.HBM)
            for a in (
                out_grads, in_acts.T, routes.T, seq_ids.reshape(1, -1), query_out[0], query_in[0].T,
                out_basis[0], in_basis[0], eigvals[0],
            )
        )
    )


def solution(mesh):
    return jax.shard_map(
        on_device,
        mesh=mesh,
        in_specs=(
            P("expert", "basis"),
            P("expert", "basis"),
            P("expert", None),
            P("expert"),
            P("expert", None, "basis"),
            P("expert", None, "basis"),
            P("expert", "basis", None),
            P("expert", "basis", None),
            P("expert", "basis", None),
        ),
        out_specs=P(None, "basis"),
        check_vma=False,
    )
```
